256 devices in a mesh: row: 16 (over x_lo, y, core), col: 16 (over x_hi, z).
Axes of the slice: x: 4 (x_hi: 2, x_lo: 2; x = x_hi * 2 + x_lo), y: 4, z: 8, core: 2. Of those that a mesh axis runs over, the one named last changes fastest.
Arguments:
- queries: bfloat16 [4096, 8192], P('row', 'col'), may hold values from -96 to 96
- keys: bfloat16 [4096, 1024], P('row'), may hold values from -4.05 to 4.05
- values: bfloat16 [4096, 1024], P('row'), may hold values from -4 to 4
- grad_attn: bfloat16 [4096, 8192], P('row', 'col'), may hold values from -12 to 12
- segment_ids: int32 [4096], replicated, may hold values from 0 to 3, as said below
- q_weight: bfloat16 [8192, 8192], P('row', 'col'), may hold values from -0.0625 to 0.0625
Outputs:
- input_grad: bfloat16 [4096, 8192], P('row', 'col')
- key_grad: bfloat16 [4096, 1024], P('row')
- value_grad: bfloat16 [4096, 1024], P('row')
The draws below stay inside these ranges and needn't reach their ends.
Inputs may be any that keep to these rules, and one draw needn't show every extreme that they name: `segment_ids`: document numbers never fall along the sequence; a document holds 1 to 2048 positions; the last document holds exactly the last 2048 positions.
All inputs are finite; a program needn't handle non-finite values.
Results may differ from the reference program's by a relative error of at most 0.015.
Values may be sent and summed in bfloat16 or wider, within the bound.
A program may use at most 64 MiB of HBM per device.

```python
import math
import jax
import jax.numpy as jnp
from jax import lax

D = 8192
H = 64
KVH = 8
HD = 128
TOK_DEV = 256
TOKENS = 4096


def draw_both(key):
    key_keys = jax.random.fold_in(key, 101)
    key_query = jax.random.fold_in(key, 202)
    base_keys = jnp.clip(jax.random.normal(key_keys, (TOKENS, KVH * HD), jnp.float32), -4.0, 4.0)
    base_query = jnp.clip(jax.random.normal(key_query, (TOKENS, H * HD), jnp.float32), -4.0, 4.0)
    keys_out = base_keys
    query_out = base_query
    return (query_out, keys_out)


def draw_queries(key, part):
    return draw_both(key)[0].astype(jnp.bfloat16)


def draw_keys(key, part):
    return draw_both(key)[1].astype(jnp.bfloat16)


def draw_segment_ids(key, part):
    half_len = TOKENS // 2
    order = jax.random.permutation(jax.random.fold_in(key, 404), half_len - 1)
    first_cut = jnp.minimum(order[0], order[1]).astype(jnp.int32) + 1
    second_cut = jnp.maximum(order[0], order[1]).astype(jnp.int32) + 1
    places = jnp.arange(TOKENS, dtype=jnp.int32)
    seg = (places >= first_cut).astype(jnp.int32) + (places >= second_cut).astype(jnp.int32) + (places >= half_len).astype(jnp.int32)
    return seg.astype(jnp.int32)


def level_of(rng, shape, shards, smallest, top_value):
    def one(axis_at, blocks):
        heights = jax.random.uniform(jax.random.fold_in(jax.random.fold_in(rng, 6), axis_at), (blocks,), jnp.float32, smallest / len(shards), top_value / len(shards))
        return jnp.repeat(jnp.exp(heights), shape[axis_at] // blocks).reshape((-1,) + (1,) * (len(shape) - axis_at - 1))

    loudness = one(*shards[0])
    for cut in shards[1:]:
        loudness = loudness * one(*cut)
    return loudness


def noise(key, shape, scale, reach, split=(), kind=jnp.bfloat16):
    array = scale * jax.random.normal(key, shape, jnp.float32)
    if split:
        array = array * level_of(key, shape, split, -0.22, 0.18)
    return jnp.clip(array, -reach, reach).astype(kind)


def setup_inputs(seed: int = 0) -> dict:
    arg_keys = jax.random.split(jax.random.key(seed), 7)
    queries = draw_queries(jax.random.fold_in(arg_keys[6], 71), 0)
    keys = draw_keys(jax.random.fold_in(arg_keys[6], 71), 0)
    values = noise(arg_keys[2], (TOKENS, KVH * HD), 1.0, 4.0, ((0, 16),))
    grad_attn = noise(arg_keys[3], (TOKENS, H * HD), 2.0, 12.0, ((0, 16), (1, 16)))
    segment_ids = draw_segment_ids(jax.random.fold_in(arg_keys[6], 71), 0)
    q_weight = noise(arg_keys[5], (H * HD, D), D ** -0.5, 0.0625, ((0, 16), (1, 16)))
    return {"queries": queries, "keys": keys, "values": values, "grad_attn": grad_attn, "segment_ids": segment_ids, "q_weight": q_weight}


def reference(queries, keys, values, grad_attn, segment_ids, q_weight):
    inv_root = 1.0 / math.sqrt(HD)
    group_size = H // KVH
    half_rows = TOK_DEV // 2
    rows_all = jnp.arange(TOKENS, dtype=jnp.int32)
    shard_of = rows_all // TOK_DEV
    local_of = rows_all % TOK_DEV
    places = jnp.where(local_of < half_rows, shard_of * half_rows + local_of, TOKENS - (shard_of + 1) * half_rows + local_of - half_rows).astype(jnp.int32)
    segs = segment_ids[places]
    allowed = (places[None, :] <= places[:, None]) & (segs[None, :] == segs[:, None])
    query_heads = queries.reshape(TOKENS, H, HD).transpose(1, 0, 2)
    grad_heads = grad_attn.reshape(TOKENS, H, HD).transpose(1, 0, 2)
    key_heads = keys.reshape(TOKENS, KVH, HD).transpose(1, 0, 2)
    value_heads = values.reshape(TOKENS, KVH, HD).transpose(1, 0, 2)

    def one_head(head_index):
        query_h = query_heads[head_index]
        grad_h = grad_heads[head_index]
        key_h = key_heads[head_index // group_size]
        value_h = value_heads[head_index // group_size]
        scores = jnp.dot(query_h, key_h.T, preferred_element_type=jnp.float32) * inv_root
        masked = jnp.where(allowed, scores, -jnp.inf)
        row_top = lax.optimization_barrier(jnp.max(masked, axis=1, keepdims=True))
        row_sum = lax.optimization_barrier(jnp.sum(jnp.exp(masked - row_top), axis=1, keepdims=True))
        row_lse = row_top + jnp.log(row_sum)
        softmax_w = jnp.where(allowed, jnp.exp(masked - row_lse), 0.0)
        grad_prob = jnp.dot(grad_h, value_h.T, preferred_element_type=jnp.float32)
        prob_dot = lax.optimization_barrier(jnp.sum(softmax_w * grad_prob, axis=1, keepdims=True))
        dscore = (softmax_w * (grad_prob - prob_dot)).astype(jnp.bfloat16)
        soft_low = softmax_w.astype(jnp.bfloat16)
        query_part = jnp.dot(dscore, key_h, preferred_element_type=jnp.float32) * inv_root
        key_part = jnp.dot(dscore.T, query_h, preferred_element_type=jnp.float32) * inv_root
        value_part = jnp.dot(soft_low.T, grad_h, preferred_element_type=jnp.float32)
        return (query_part, key_part, value_part)
    query_parts, key_parts, value_parts = lax.map(one_head, jnp.arange(H, dtype=jnp.int32))
    key_sum = key_parts.reshape(KVH, group_size, TOKENS, HD).sum(axis=1)
    value_sum = value_parts.reshape(KVH, group_size, TOKENS, HD).sum(axis=1)
    key_grad = key_sum.transpose(1, 0, 2).reshape(TOKENS, KVH * HD).astype(jnp.bfloat16)
    value_grad = value_sum.transpose(1, 0, 2).reshape(TOKENS, KVH * HD).astype(jnp.bfloat16)
    query_grad = query_parts.transpose(1, 0, 2).reshape(TOKENS, H * HD).astype(jnp.bfloat16)
    input_grad = jnp.dot(query_grad, q_weight, preferred_element_type=jnp.float32).astype(jnp.bfloat16)
    return (input_grad, key_grad, value_grad)
```

```python
import functools
import math

import jax
import jax.numpy as jnp
from jax import lax
from jax.experimental import pallas as pl
from jax.experimental.pallas import tpu as pltpu
from jax.sharding import PartitionSpec as P

H = 64
KVH = 8
HD = 128
TOKENS = 4096
HALF = 128
PER = 4
NEG = -1e30
MESH = pl.DeviceIdType.MESH
INV_ROOT = 1.0 / math.sqrt(HD)
SCALE2 = INV_ROOT * math.log2(math.e)
F32 = jnp.float32
BF16 = jnp.bfloat16


def dot_nt(a, b):
    return lax.dot_general(a, b, (((1,), (1,)), ((), ())), preferred_element_type=F32)


def dot_nn(a, b):
    return lax.dot_general(a, b, (((1,), (0,)), ((), ())), preferred_element_type=F32)


def dot_tn(a, b):
    return lax.dot_general(a, b, (((0,), (0,)), ((), ())), preferred_element_type=F32)


def attention_kernel(
    q_ref, k_hbm, v_hbm, g_ref, seg_ref,
    wide_hbm, kout_ref, vout_ref,
    kvbuf, sbuf, dpbuf, q4, g4, dq4, stat, pbuf, rbuf, ownf, pair_s, pair_r, dqbuf, pieces,
    load_sem, kv_send, kv_recv, fw_send, fw_recv, dkv_send, dkv_recv, pair_sem,
    xq_send, xq_recv, xp_sem, z_send, z_recv, p_send, p_recv, out_sem,
):
    s = lax.axis_index("row")
    j = lax.axis_index("col")
    chip, core = s // 2, s % 2
    xh, z = j // 8, j % 8
    sibling = s + 1 - 2 * core
    partner = (1 - xh) * 8 + z
    right = xh * 8 + (z + 1) % 8
    left = xh * 8 + (z + 7) % 8
    parity = z % 2
    mate = j + 1 - 2 * parity
    head = j // 2

    def remote(src, dst, ssem, rsem, row, col):
        return pltpu.make_async_remote_copy(
            src_ref=src, dst_ref=dst, send_sem=ssem, recv_sem=rsem,
            device_id=(row, col), device_id_type=MESH,
        )

    lanes = pl.ds(pl.multiple_of(head * HD, HD), HD)
    loads = []
    for u in range(2):
        slot = s if u == 0 else 16
        for i, ref in enumerate((k_hbm, v_hbm)):
            loads.append(
                pltpu.make_async_copy(
                    ref.at[pl.ds(u * HALF, HALF), lanes], kvbuf.at[slot, i], load_sem.at[2 * u + i]
                )
            )
    for copy in loads:
        copy.start()

    barrier = pltpu.get_barrier_semaphore()

    def greet(e, carry):
        pl.semaphore_signal(barrier, inc=1, device_id=((s + e) % 16, j), device_id_type=MESH)
        return carry

    lax.fori_loop(1, 16, greet, 0)
    for col in (right, left, partner):
        pl.semaphore_signal(barrier, inc=1, device_id=(s, col), device_id_type=MESH)

    for u in range(2):
        for h in range(PER):
            q4[u, h * HD:(h + 1) * HD, :] = q_ref[u * HALF:(u + 1) * HALF, h * HD:(h + 1) * HD]
            g4[u, h * HD:(h + 1) * HD, :] = g_ref[u * HALF:(u + 1) * HALF, h * HD:(h + 1) * HD]

    seg = seg_ref[...]
    counts = [jnp.sum((seg < v).astype(F32), keepdims=True) for v in (1, 2, 3)]
    lane = lax.broadcasted_iota(jnp.int32, (1, HALF), 1).astype(F32)
    bounds = []
    for u in range(2):
        block = s if u == 0 else 31 - s
        seg_q = seg_ref[pl.ds(block, 1), :]
        start = jnp.where(
            seg_q == 0, 0.0,
            jnp.where(seg_q == 1, counts[0], jnp.where(seg_q == 2, counts[1], counts[2])),
        )
        stat[4 + u, 0:1, 0:HALF] = start
        stat[4 + u, 1:2, 0:HALF] = lane + (block * HALF).astype(F32)
        stat[u] = jnp.full((8, PER * HALF), NEG, F32)

    for copy in loads:
        copy.wait()
    pl.semaphore_wait(barrier, 18)

    def kv_copy(d, chip_to, row_to):
        src = kvbuf.at[jnp.where(chip_to > chip, s, 16)]
        return remote(src, kvbuf.at[s], kv_send.at[d], kv_recv.at[d], row_to, j)

    def kv_out(d):
        chip_to = (chip + d) % 8
        return kv_copy(d, chip_to, chip_to * 2 + core)

    def kv_start(d, carry):
        kv_out(d).start()
        return carry

    own_half = kvbuf.at[jnp.where(core == 0, s, 16)]
    to_sibling = remote(own_half, kvbuf.at[s], kv_send.at[0], kv_recv.at[0], sibling, j)
    lax.fori_loop(1, 8, kv_start, 0)
    to_sibling.start()

    sub = lax.broadcasted_iota(jnp.int32, (HALF, HALF), 0).astype(F32)

    def pass_one(t):
        u = jnp.where(t > s, 1, 0)
        block = jnp.where(t > s, jnp.where(t == 16, 31 - s, 31 - t), t)
        key_place = sub + (block * HALF).astype(F32)
        start = stat[4 + u, 0:1, 0:HALF]
        place = stat[4 + u, 1:2, 0:HALF]
        bias = jnp.where((key_place >= start) & (key_place <= place), 0.0, NEG)
        scores = dot_nt(kvbuf[t, 0], q4[u])
        for h in range(PER):
            part = scores[:, h * HALF:(h + 1) * HALF] * SCALE2 + bias
            sbuf[t, :, h * HALF:(h + 1) * HALF] = part
            top = jnp.max(part.reshape(16, 8, HALF), axis=0)
            stat[u, :, h * HALF:(h + 1) * HALF] = jnp.maximum(
                stat[u, :, h * HALF:(h + 1) * HALF], top
            )
        dpbuf[t] = dot_nt(kvbuf[t, 1], g4[u])

    pass_one(s)
    pass_one(16)

    def forward(d):
        origin = ((chip + 8 - d) % 8) * 2 + core
        return remote(kvbuf.at[origin], kvbuf.at[origin], fw_send.at[d], fw_recv.at[d], sibling, j)

    def arrive(d, carry):
        origin = ((chip + 8 - d) % 8) * 2 + core
        remote(
            kvbuf.at[origin], kvbuf.at[origin], kv_send.at[d], kv_recv.at[d], sibling, j
        ).wait_recv()
        forward(d).start()
        pass_one(origin)
        return carry

    lax.fori_loop(1, 8, arrive, 0)
    remote(
        kvbuf.at[sibling], kvbuf.at[sibling], kv_send.at[0], kv_recv.at[0], sibling, j
    ).wait_recv()
    pass_one(sibling)

    def arrive_two(d, carry):
        origin = ((chip + 8 - d) % 8) * 2 + 1 - core
        remote(
            kvbuf.at[origin], kvbuf.at[origin], fw_send.at[d], fw_recv.at[d], sibling, j
        ).wait_recv()
        pass_one(origin)
        return carry

    lax.fori_loop(1, 8, arrive_two, 0)

    for u in range(2):
        top = jnp.max(stat[u], axis=0, keepdims=True)
        stat[u] = jnp.broadcast_to(top, (8, PER * HALF))
        stat[2 + u] = jnp.zeros((8, PER * HALF), F32)
        stat[6 + u] = jnp.zeros((8, PER * HALF), F32)

    def pass_two(t, carry):
        u = jnp.where(t > s, 1, 0)
        for h in range(PER):
            cols = slice(h * HALF, (h + 1) * HALF)
            top = stat[u, 0:1, cols]
            expo = jnp.exp2(sbuf[t, :, cols] - top)
            sbuf[t, :, cols] = expo
            stat[2 + u, :, cols] += jnp.sum(expo.reshape(16, 8, HALF), axis=0)
            stat[6 + u, :, cols] += jnp.sum((expo * dpbuf[t, :, cols]).reshape(16, 8, HALF), axis=0)
        return carry

    lax.fori_loop(0, 17, pass_two, 0)
    for u in range(2):
        total = jnp.sum(stat[2 + u], axis=0, keepdims=True)
        inverse = 1.0 / total
        delta = jnp.sum(stat[6 + u], axis=0, keepdims=True) * inverse
        stat[2 + u, 0:1, :] = inverse
        stat[6 + u, 0:1, :] = delta
        dq4[u] = jnp.zeros((PER * HALF, HD), F32)

    def dkv_out(t):
        return remote(pbuf.at[t], rbuf.at[s], dkv_send.at[t], dkv_recv.at[s], t, j)

    def pass_three(t, carry):
        u = jnp.where(t > s, 1, 0)
        inverse = stat[2 + u, 0:1, :]
        delta = stat[6 + u, 0:1, :]
        probs = sbuf[t] * inverse
        dscore = (probs * (dpbuf[t] - delta)).astype(BF16)
        key_part = dot_nn(dscore, q4[u])
        value_part = dot_nn(probs.astype(BF16), g4[u])
        dq4[u] += dot_tn(dscore, kvbuf[t, 0])
        mine = (t == s) | (t == 16)

        @pl.when(mine)
        def _():
            ownf[u, 0] = key_part
            ownf[u, 1] = value_part

        @pl.when(jnp.logical_not(mine))
        def _():
            pbuf[t, 0] = key_part.astype(BF16)
            pbuf[t, 1] = value_part.astype(BF16)
            dkv_out(t).start()

        return carry

    def x_copy(u):
        rows = pl.ds(u * HALF, HALF)
        src = dqbuf.at[xh, z, rows]
        return remote(src, src, xq_send.at[u], xq_recv.at[u], s, partner)

    def x_wait(u):
        dst = dqbuf.at[1 - xh, z, pl.ds(u * HALF, HALF)]
        remote(dst, dst, xq_send.at[u], xq_recv.at[u], s, partner).wait_recv()

    def z_copy(way, k, e, u):
        origin = (z + 8 - (k - 1)) % 8 if way == 0 else (z + (k - 1)) % 8
        side = xh if e == 0 else 1 - xh
        src = dqbuf.at[side, origin, pl.ds(u * HALF, HALF)]
        index = ((way * 4 + (k - 1)) * 2 + e) * 2 + u
        return remote(src, src, z_send.at[index], z_recv.at[index], s, right if way == 0 else left)

    def z_wait(way, k, e, u):
        origin = (z + 8 - k) % 8 if way == 0 else (z + k) % 8
        side = xh if e == 0 else 1 - xh
        dst = dqbuf.at[side, origin, pl.ds(u * HALF, HALF)]
        index = ((way * 4 + (k - 1)) * 2 + e) * 2 + u
        remote(dst, dst, z_send.at[index], z_recv.at[index], s, right).wait_recv()

    def hops(way, k, u):
        return k <= 3 or u == way

    def z_turn(k, e):
        for u in (1, 0):
            for way in range(2):
                if hops(way, k, u):
                    z_wait(way, k, e, u)
                    if k < 4 and hops(way, k + 1, u):
                        z_copy(way, k + 1, e, u).start()

    for u, first, last in ((1, s + 1, 17), (0, 0, s + 1)):
        lax.fori_loop(first, last, pass_three, 0)
        for h in range(PER):
            dqbuf[xh, z, u * HALF:(u + 1) * HALF, h * HD:(h + 1) * HD] = (
                dq4[u, h * HD:(h + 1) * HD, :] * INV_ROOT
            ).astype(BF16)
        z_copy(0, 1, 0, u).start()
        z_copy(1, 1, 0, u).start()
        x_copy(u).start()

    def spread(side, origin):
        lanes = pl.ds(pl.multiple_of((side * 8 + origin) * 512, 512), 512)
        return pltpu.make_async_copy(
            dqbuf.at[side, origin], wide_hbm.at[:, lanes], out_sem.at[side, origin]
        )

    z_turn(1, 0)
    for u in (1, 0):
        x_wait(u)
        z_copy(0, 1, 1, u).start()
        z_copy(1, 1, 1, u).start()
    z_turn(2, 0)

    def dkv_wait(r, carry):
        remote(rbuf.at[r], rbuf.at[r], dkv_send.at[r], dkv_recv.at[r], s, right).wait_recv()
        return carry

    lax.fori_loop(0, s, dkv_wait, 0)
    lax.fori_loop(s + 1, 16, dkv_wait, 0)

    def add_to(u):
        def add(r, carry):
            for i in range(2):
                ownf[u, i] += rbuf[r, i].astype(F32)
            return carry
        return add

    lax.fori_loop(s + 1, 16, add_to(0), 0)
    lax.fori_loop(0, s, add_to(1), 0)
    for u in range(2):
        pair_s[u * HALF:(u + 1) * HALF, :] = ownf[u, 1 - parity].astype(BF16)
    pair_copy = remote(pair_s, pair_r, pair_sem.at[0], pair_sem.at[1], s, mate)
    pair_copy.start()

    z_turn(1, 1)
    z_turn(3, 0)

    pair_copy.wait_recv()
    factor = jnp.where(parity == 0, INV_ROOT, 1.0).astype(F32)
    for u in range(2):
        rows = slice(u * HALF, (u + 1) * HALF)
        pieces[z, xh, rows, :] = (
            (ownf[u, parity] + pair_r[rows, :].astype(F32)) * factor
        ).astype(BF16)
    piece = pieces.at[z, xh]
    piece_copy = remote(piece, piece, xp_sem.at[0], xp_sem.at[1], s, partner)
    piece_copy.start()

    z_turn(2, 1)
    z_turn(4, 0)
    other = pieces.at[z, 1 - xh]
    remote(other, other, xp_sem.at[0], xp_sem.at[1], s, partner).wait_recv()

    def p_copy(way, k, i):
        origin = (z + 8 - (k - 1)) % 8 if way == 0 else (z + (k - 1)) % 8
        src = pieces.at[origin, i]
        index = (way * 4 + (k - 1)) * 2 + i
        return remote(src, src, p_send.at[index], p_recv.at[index], s, right if way == 0 else left)

    def p_wait(way, k, i):
        origin = (z + 8 - k) % 8 if way == 0 else (z + k) % 8
        dst = pieces.at[origin, i]
        index = (way * 4 + (k - 1)) * 2 + i
        remote(dst, dst, p_send.at[index], p_recv.at[index], s, right).wait_recv()

    for i in range(2):
        p_copy(0, 1, i).start()
        p_copy(1, 1, i).start()
    z_turn(3, 1)

    def p_turn(k):
        for i in (1, 0):
            for way in range(2):
                if hops(way, k, i):
                    p_wait(way, k, i)
                    if k < 4 and hops(way, k + 1, i):
                        p_copy(way, k + 1, i).start()

    p_turn(1)
    z_turn(4, 1)
    for side in range(2):
        for origin in range(8):
            spread(side, origin).start()
    p_turn(2)
    p_turn(3)
    p_turn(4)
    for g in range(KVH):
        cols = slice(g * HD, (g + 1) * HD)
        kout_ref[:, cols] = pieces[2 * (g % 4), g // 4]
        vout_ref[:, cols] = pieces[2 * (g % 4) + 1, g // 4]

    def kv_done(d, carry):
        kv_out(d).wait_send()
        forward(d).wait_send()
        return carry

    lax.fori_loop(1, 8, kv_done, 0)
    to_sibling.wait_send()

    def dkv_done(t, carry):
        dkv_out(t).wait_send()
        return carry

    lax.fori_loop(0, s, dkv_done, 0)
    lax.fori_loop(s + 1, 16, dkv_done, 0)
    pair_copy.wait_send()
    piece_copy.wait_send()
    for u in range(2):
        x_copy(u).wait_send()
    for way in range(2):
        for k in range(1, 5):
            for u in range(2):
                if hops(way, k, u):
                    for e in range(2):
                        z_copy(way, k, e, u).wait_send()
                    p_copy(way, k, u).wait_send()
    for side in range(2):
        for origin in range(8):
            spread(side, origin).wait()


def local(queries, keys, values, grad_attn, segment_ids, q_weight):
    rows, width = queries.shape
    vmem = pl.BlockSpec(memory_space=pltpu.VMEM)
    anywhere = pl.BlockSpec(memory_space=pl.ANY)
    dma = pltpu.SemaphoreType.DMA
    weight = lax.all_gather(q_weight, "row", axis=0, tiled=True)
    wide, key_grad, value_grad = pl.pallas_call(
        attention_kernel,
        out_shape=(
            jax.ShapeDtypeStruct((rows, H * HD), BF16),
            jax.ShapeDtypeStruct((rows, KVH * HD), BF16),
            jax.ShapeDtypeStruct((rows, KVH * HD), BF16),
        ),
        in_specs=[vmem, anywhere, anywhere, vmem, vmem],
        out_specs=(anywhere, vmem, vmem),
        scratch_shapes=[
            pltpu.VMEM((17, 2, HALF, HD), BF16),
            pltpu.VMEM((17, HALF, PER * HALF), F32),
            pltpu.VMEM((17, HALF, PER * HALF), F32),
            pltpu.VMEM((2, PER * HALF, HD), BF16),
            pltpu.VMEM((2, PER * HALF, HD), BF16),
            pltpu.VMEM((2, PER * HALF, HD), F32),
            pltpu.VMEM((8, 8, PER * HALF), F32),
            pltpu.VMEM((16, 2, HALF, HD), BF16),
            pltpu.VMEM((16, 2, HALF, HD), BF16),
            pltpu.VMEM((2, 2, HALF, HD), F32),
            pltpu.VMEM((2 * HALF, HD), BF16),
            pltpu.VMEM((2 * HALF, HD), BF16),
            pltpu.VMEM((2, 8, 2 * HALF, PER * HD), BF16),
            pltpu.VMEM((8, 2, 2 * HALF, HD), BF16),
            dma((4,)), dma((8,)), dma((8,)), dma((8,)), dma((8,)), dma((16,)), dma((16,)), dma((2,)),
            dma((2,)), dma((2,)), dma((2,)), dma((32,)), dma((32,)), dma((16,)), dma((16,)),
            dma((2, 8)),
        ],
        compiler_params=pltpu.CompilerParams(
            collective_id=0, has_side_effects=True, vmem_limit_bytes=40 * 1024 * 1024
        ),
        cost_estimate=pl.CostEstimate(
            flops=2 * 17 * 5 * 128 * 128 * 512, bytes_accessed=200_000_000, transcendentals=17 * 128 * 512
        ),
    )(queries, keys, values, grad_attn, segment_ids.reshape(32, 128))
    input_sum = jnp.dot(wide, weight, preferred_element_type=F32)
    return (input_sum.astype(BF16), key_grad, value_grad)


def solution(mesh):
    placed = (
        P("row", "col"),
        P("row", None),
        P("row", None),
        P("row", "col"),
        P(),
        P("row", "col"),
    )
    return jax.shard_map(
        local,
        mesh=mesh,
        in_specs=placed,
        out_specs=(P("row", "col"), P("row", None), P("row", None)),
        check_vma=False,
    )
```

```python
import functools
import math

import jax
import jax.numpy as jnp
from jax import lax
from jax.experimental import pallas as pl
from jax.experimental.pallas import tpu as pltpu
from jax.sharding import PartitionSpec as P

H = 64
KVH = 8
HD = 128
TOKENS = 4096
HALF = 128
PER = 4
NEG = -1e30
MESH = pl.DeviceIdType.MESH
INV_ROOT = 1.0 / math.sqrt(HD)
SCALE2 = INV_ROOT * math.log2(math.e)
F32 = jnp.float32
BF16 = jnp.bfloat16


def dot_nt(a, b):
    return lax.dot_general(a, b, (((1,), (1,)), ((), ())), preferred_element_type=F32)


def dot_nn(a, b):
    return lax.dot_general(a, b, (((1,), (0,)), ((), ())), preferred_element_type=F32)


def dot_tn(a, b):
    return lax.dot_general(a, b, (((0,), (0,)), ((), ())), preferred_element_type=F32)


def attention_kernel(
    q_ref, k_hbm, v_hbm, g_ref, seg_ref, w_hbm,
    out_ref, kout_ref, vout_ref,
    kvbuf, sbuf, dpbuf, q4, g4, dq4, stat, pbuf, mbuf, rbuf, ownf, pair_s, pair_r, dqbuf, pieces,
    wbuf, acc, part_s, part_r,
    load_sem, kv_send, kv_recv, fw_send, fw_recv, m_send, m_recv, dkv_send, dkv_recv, pair_sem,
    xp_sem, z_send, z_recv, p_send, p_recv,
    wl_sem, wx_send, wx_recv, wy_send, wy_recv, wf_send, wf_recv, ws_send, ws_recv, c_send, c_recv,
):
    s = lax.axis_index("row")
    j = lax.axis_index("col")
    chip, core = s // 2, s % 2
    xl, y = chip // 4, chip % 4
    xh, z = j // 8, j % 8
    sibling = s + 1 - 2 * core
    partner = (1 - xh) * 8 + z
    right = xh * 8 + (z + 1) % 8
    left = xh * 8 + (z + 7) % 8
    parity = z % 2
    mate = j + 1 - 2 * parity
    head = j // 2
    inner = xl != xh
    outer = xl == xh

    def remote(src, dst, ssem, rsem, row, col):
        return pltpu.make_async_remote_copy(
            src_ref=src, dst_ref=dst, send_sem=ssem, recv_sem=rsem,
            device_id=(row, col), device_id_type=MESH,
        )

    lanes = pl.ds(pl.multiple_of(head * HD, HD), HD)
    loads = []
    for u in range(2):
        slot = s if u == 0 else 16
        for i, ref in enumerate((k_hbm, v_hbm)):
            loads.append(
                pltpu.make_async_copy(
                    ref.at[pl.ds(u * HALF, HALF), lanes], kvbuf.at[slot, i], load_sem.at[2 * u + i]
                )
            )
    for copy in loads:
        copy.start()

    barrier = pltpu.get_barrier_semaphore()

    def greet(e, carry):
        pl.semaphore_signal(barrier, inc=1, device_id=((s + e) % 16, j), device_id_type=MESH)
        return carry

    lax.fori_loop(1, 16, greet, 0)
    across = (1 - xl) * 8 + y * 2 + core
    for row, col in ((s, right), (s, left), (s, partner), (across, partner)):
        pl.semaphore_signal(barrier, inc=1, device_id=(row, col), device_id_type=MESH)

    for u in range(2):
        for h in range(PER):
            q4[u, h * HD:(h + 1) * HD, :] = q_ref[u * HALF:(u + 1) * HALF, h * HD:(h + 1) * HD]
            g4[u, h * HD:(h + 1) * HD, :] = g_ref[u * HALF:(u + 1) * HALF, h * HD:(h + 1) * HD]

    seg = seg_ref[...]
    counts = [jnp.sum((seg < v).astype(F32), keepdims=True) for v in (1, 2, 3)]
    lane = lax.broadcasted_iota(jnp.int32, (1, HALF), 1).astype(F32)
    bounds = []
    for u in range(2):
        block = s if u == 0 else 31 - s
        seg_q = seg_ref[pl.ds(block, 1), :]
        start = jnp.where(
            seg_q == 0, 0.0,
            jnp.where(seg_q == 1, counts[0], jnp.where(seg_q == 2, counts[1], counts[2])),
        )
        stat[4 + u, 0:1, 0:HALF] = start
        stat[4 + u, 1:2, 0:HALF] = lane + (block * HALF).astype(F32)
        stat[u] = jnp.full((8, PER * HALF), NEG, F32)

    for copy in loads:
        copy.wait()
    pl.semaphore_wait(barrier, 19)

    def kv_copy(d, chip_to, row_to):
        src = kvbuf.at[jnp.where(chip_to > chip, s, 16)]
        return remote(src, kvbuf.at[s], kv_send.at[d], kv_recv.at[d], row_to, j)

    def kv_out(d):
        chip_to = (chip + d) % 8
        return kv_copy(d, chip_to, chip_to * 2 + core)

    def kv_start(d, carry):
        kv_out(d).start()
        return carry

    own_half = kvbuf.at[jnp.where(core == 0, s, 16)]
    to_sibling = remote(own_half, kvbuf.at[s], kv_send.at[0], kv_recv.at[0], sibling, j)
    lax.fori_loop(1, 8, kv_start, 0)
    to_sibling.start()

    slot = 2 * y + core
    own_weight = pltpu.make_async_copy(w_hbm, wbuf.at[slot, xh], wl_sem.at[0])
    weight_x = remote(
        w_hbm, wbuf.at[slot, xh], wx_send.at[0], wx_recv.at[xh], across, xl * 8 + z
    )
    weight_on = remote(
        wbuf.at[slot, 1 - xh], wbuf.at[slot, 1 - xh], wx_send.at[1], wx_recv.at[1 - xh], across, j
    )
    weight_x.start()
    pl.when(outer)(own_weight.start)

    def slot_at(step, which):
        return 2 * ((y + step) % 4) + which

    def row_at(step):
        return xl * 8 + ((y + step) % 4) * 2 + core

    def weight_arrived(e):
        ref = wbuf.at[slot, e]
        remote(ref, ref, wx_send.at[0], wx_recv.at[e], across, j).wait_recv()

    def y_copy(e, way):
        ref = wbuf.at[slot, e]
        index = 2 * e + way
        return remote(ref, ref, wy_send.at[index], wy_recv.at[index], row_at(3 if way else 1), j)

    def y_wait(e, way):
        ref = wbuf.at[slot_at(1 if way else 3, core), e]
        index = 2 * e + way
        remote(ref, ref, wy_send.at[index], wy_recv.at[index], s, right).wait_recv()

    def f_ref(step, e, way):
        return wbuf.at[slot_at(step, core), e, pl.ds(way * 256, 256)]

    def f_copy(e, way):
        ref = f_ref(1 if way else 3, e, way)
        index = 2 * e + way
        return remote(ref, ref, wf_send.at[index], wf_recv.at[index], row_at(3 if way else 1), j)

    def f_wait(e, way):
        ref = f_ref(2, e, way)
        index = 2 * e + way
        remote(ref, ref, wf_send.at[index], wf_recv.at[index], s, right).wait_recv()

    def s_copy(e, i, which):
        if i < 3:
            ref = wbuf.at[slot_at((0, 3, 1)[i], which), e]
        else:
            ref = wbuf.at[slot_at(2, which), e, pl.ds((i - 3) * 256, 256)]
        index = 5 * e + i
        return remote(ref, ref, ws_send.at[index], ws_recv.at[index], sibling, j)

    def weight_start(e):
        y_copy(e, 0).start()
        y_copy(e, 1).start()
        s_copy(e, 0, core).start()

    def weight_pass(e):
        for way in range(2):
            y_wait(e, way)
            f_copy(e, way).start()
            s_copy(e, 1 + way, core).start()

    def weight_last(e):
        for way in range(2):
            f_wait(e, way)
            s_copy(e, 3 + way, core).start()

    def weight_ready(e):
        for i in range(5):
            s_copy(e, i, 1 - core).wait_recv()

    sub = lax.broadcasted_iota(jnp.int32, (HALF, HALF), 0).astype(F32)

    def pass_one(t):
        u = jnp.where(t > s, 1, 0)
        block = jnp.where(t > s, jnp.where(t == 16, 31 - s, 31 - t), t)
        key_place = sub + (block * HALF).astype(F32)
        start = stat[4 + u, 0:1, 0:HALF]
        place = stat[4 + u, 1:2, 0:HALF]
        bias = jnp.where((key_place >= start) & (key_place <= place), 0.0, NEG)
        scores = dot_nt(kvbuf[t, 0], q4[u])
        for h in range(PER):
            part = scores[:, h * HALF:(h + 1) * HALF] * SCALE2 + bias
            sbuf[t, :, h * HALF:(h + 1) * HALF] = part
            top = jnp.max(part.reshape(16, 8, HALF), axis=0)
            stat[u, :, h * HALF:(h + 1) * HALF] = jnp.maximum(
                stat[u, :, h * HALF:(h + 1) * HALF], top
            )
        dpbuf[t] = dot_nt(kvbuf[t, 1], g4[u])

    pass_one(s)
    pass_one(16)

    def forward(d):
        origin = ((chip + 8 - d) % 8) * 2 + core
        return remote(kvbuf.at[origin], kvbuf.at[origin], fw_send.at[d], fw_recv.at[d], sibling, j)

    def arrive(d, carry):
        origin = ((chip + 8 - d) % 8) * 2 + core
        remote(
            kvbuf.at[origin], kvbuf.at[origin], kv_send.at[d], kv_recv.at[d], sibling, j
        ).wait_recv()
        forward(d).start()
        pass_one(origin)
        return carry

    lax.fori_loop(1, 8, arrive, 0)

    @pl.when(inner)
    def _():
        weight_arrived(xh)

    @pl.when(outer)
    def _():
        own_weight.wait()

    weight_start(xh)
    remote(
        kvbuf.at[sibling], kvbuf.at[sibling], kv_send.at[0], kv_recv.at[0], sibling, j
    ).wait_recv()
    pass_one(sibling)

    def arrive_two(d, carry):
        origin = ((chip + 8 - d) % 8) * 2 + 1 - core
        remote(
            kvbuf.at[origin], kvbuf.at[origin], fw_send.at[d], fw_recv.at[d], sibling, j
        ).wait_recv()
        pass_one(origin)
        return carry

    lax.fori_loop(1, 8, arrive_two, 0)

    @pl.when(inner)
    def _():
        weight_arrived(1 - xh)
        weight_on.start()
        weight_start(1 - xh)

    for u in range(2):
        top = jnp.max(stat[u], axis=0, keepdims=True)
        stat[u] = jnp.broadcast_to(top, (8, PER * HALF))
        stat[2 + u] = jnp.zeros((8, PER * HALF), F32)
        stat[6 + u] = jnp.zeros((8, PER * HALF), F32)

    def pass_two(t, carry):
        u = jnp.where(t > s, 1, 0)
        for h in range(PER):
            cols = slice(h * HALF, (h + 1) * HALF)
            top = stat[u, 0:1, cols]
            expo = jnp.exp2(sbuf[t, :, cols] - top)
            sbuf[t, :, cols] = expo
            stat[2 + u, :, cols] += jnp.sum(expo.reshape(16, 8, HALF), axis=0)
            stat[6 + u, :, cols] += jnp.sum((expo * dpbuf[t, :, cols]).reshape(16, 8, HALF), axis=0)
        return carry

    lax.fori_loop(0, 17, pass_two, 0)

    @pl.when(outer)
    def _():
        weight_arrived(1 - xh)
        weight_start(1 - xh)

    for u in range(2):
        total = jnp.sum(stat[2 + u], axis=0, keepdims=True)
        inverse = 1.0 / total
        delta = jnp.sum(stat[6 + u], axis=0, keepdims=True) * inverse
        stat[2 + u, 0:1, :] = inverse
        stat[6 + u, 0:1, :] = delta
        dq4[u] = jnp.zeros((PER * HALF, HD), F32)

    def m_copy(t):
        return remote(pbuf.at[t], mbuf.at[t], m_send.at[t], m_recv.at[t], sibling, j)

    def dkv_out(t):
        return remote(pbuf.at[t], rbuf.at[s], dkv_send.at[t], dkv_recv.at[s], t, j)

    def pass_three(t, carry):
        u = jnp.where(t > s, 1, 0)
        inverse = stat[2 + u, 0:1, :]
        delta = stat[6 + u, 0:1, :]
        probs = sbuf[t] * inverse
        dscore = (probs * (dpbuf[t] - delta)).astype(BF16)
        key_part = dot_nn(dscore, q4[u])
        value_part = dot_nn(probs.astype(BF16), g4[u])
        dq4[u] += dot_tn(dscore, kvbuf[t, 0])
        mine = (t == s) | (t == 16)

        @pl.when(mine)
        def _():
            ownf[u, 0] = key_part
            ownf[u, 1] = value_part

        @pl.when(jnp.logical_not(mine))
        def _():
            pbuf[t, 0] = key_part.astype(BF16)
            pbuf[t, 1] = value_part.astype(BF16)

            @pl.when(t == sibling)
            def _():
                dkv_out(t).start()

            @pl.when((t != sibling) & (t % 2 != core))
            def _():
                m_copy(t).start()

        return carry

    def z_copy(way, k, u):
        origin = (z + 8 - (k - 1)) % 8 if way == 0 else (z + (k - 1)) % 8
        src = dqbuf.at[origin, pl.ds(u * HALF, HALF)]
        index = (way * 4 + (k - 1)) * 2 + u
        return remote(src, src, z_send.at[index], z_recv.at[index], s, right if way == 0 else left)

    def z_wait(way, k, u):
        origin = (z + 8 - k) % 8 if way == 0 else (z + k) % 8
        dst = dqbuf.at[origin, pl.ds(u * HALF, HALF)]
        index = (way * 4 + (k - 1)) * 2 + u
        remote(dst, dst, z_send.at[index], z_recv.at[index], s, right).wait_recv()

    def hops(way, k, u):
        return k <= 3 or u == way

    def z_turn(k):
        for u in (1, 0):
            for way in range(2):
                if hops(way, k, u):
                    z_wait(way, k, u)
                    if k < 4 and hops(way, k + 1, u):
                        z_copy(way, k + 1, u).start()

    for u, first, last in ((1, s + 1, 17), (0, 0, s + 1)):
        lax.fori_loop(first, last, pass_three, 0)
        for h in range(PER):
            dqbuf[z, u * HALF:(u + 1) * HALF, h * HD:(h + 1) * HD] = (
                dq4[u, h * HD:(h + 1) * HD, :] * INV_ROOT
            ).astype(BF16)
        z_copy(0, 1, u).start()
        z_copy(1, 1, u).start()

    def merge(d, carry):
        t = 2 * ((chip + d) % 8) + core
        remote(pbuf.at[t], mbuf.at[t], m_send.at[t], m_recv.at[t], sibling, j).wait_recv()
        for i in range(2):
            pbuf[t, i] = (pbuf[t, i].astype(F32) + mbuf[t, i].astype(F32)).astype(BF16)
        dkv_out(t).start()
        return carry

    lax.fori_loop(1, 8, merge, 0)
    z_turn(1)
    weight_pass(xh)
    z_turn(2)

    def dkv_take(r):
        remote(rbuf.at[r], rbuf.at[r], dkv_send.at[r], dkv_recv.at[r], s, right).wait_recv()
        u = jnp.where(r > s, 0, 1)
        for i in range(2):
            ownf[u, i] += rbuf[r, i].astype(F32)

    def take(d, carry):
        dkv_take(2 * ((chip + 8 - d) % 8) + core)
        return carry

    dkv_take(sibling)
    lax.fori_loop(1, 8, take, 0)
    for u in range(2):
        pair_s[u * HALF:(u + 1) * HALF, :] = ownf[u, 1 - parity].astype(BF16)
    pair_copy = remote(pair_s, pair_r, pair_sem.at[0], pair_sem.at[1], s, mate)
    pair_copy.start()

    z_turn(3)
    weight_pass(1 - xh)

    pair_copy.wait_recv()
    factor = jnp.where(parity == 0, INV_ROOT, 1.0).astype(F32)
    for u in range(2):
        rows = slice(u * HALF, (u + 1) * HALF)
        pieces[z, xh, rows, :] = (
            (ownf[u, parity] + pair_r[rows, :].astype(F32)) * factor
        ).astype(BF16)
    piece = pieces.at[z, xh]
    piece_copy = remote(piece, piece, xp_sem.at[0], xp_sem.at[1], s, partner)
    piece_copy.start()

    z_turn(4)
    other = pieces.at[z, 1 - xh]
    remote(other, other, xp_sem.at[0], xp_sem.at[1], s, partner).wait_recv()

    def p_copy(way, k, i):
        origin = (z + 8 - (k - 1)) % 8 if way == 0 else (z + (k - 1)) % 8
        src = pieces.at[origin, i]
        index = (way * 4 + (k - 1)) * 2 + i
        return remote(src, src, p_send.at[index], p_recv.at[index], s, right if way == 0 else left)

    def p_wait(way, k, i):
        origin = (z + 8 - k) % 8 if way == 0 else (z + k) % 8
        dst = pieces.at[origin, i]
        index = (way * 4 + (k - 1)) * 2 + i
        remote(dst, dst, p_send.at[index], p_recv.at[index], s, right).wait_recv()

    for i in range(2):
        p_copy(0, 1, i).start()
        p_copy(1, 1, i).start()

    def p_turn(k):
        for i in (1, 0):
            for way in range(2):
                if hops(way, k, i):
                    p_wait(way, k, i)
                    if k < 4 and hops(way, k + 1, i):
                        p_copy(way, k + 1, i).start()

    def product(e, u):
        rows = pl.ds(u * HALF, HALF)
        acc[u] = jnp.zeros((HALF, 512), F32)

        def add(zz, carry):
            acc[u] += dot_nn(dqbuf[zz, rows, :], wbuf[zz, e])
            return carry

        lax.fori_loop(0, 8, add, 0)

    def c_copy(u):
        return remote(part_s.at[u], part_r.at[u], c_send.at[u], c_recv.at[u], s, partner)

    weight_last(1 - xh)
    weight_ready(1 - xh)
    for u in range(2):
        product(1 - xh, u)
        part_s[u] = acc[u].astype(BF16)
        c_copy(u).start()
    p_turn(1)
    weight_last(xh)
    p_turn(2)
    weight_ready(xh)
    for u in range(2):
        product(xh, u)
    p_turn(3)
    p_turn(4)
    for g in range(KVH):
        cols = slice(g * HD, (g + 1) * HD)
        kout_ref[:, cols] = pieces[2 * (g % 4), g // 4]
        vout_ref[:, cols] = pieces[2 * (g % 4) + 1, g // 4]

    for u in range(2):
        c_copy(u).wait_recv()
        out_ref[u * HALF:(u + 1) * HALF, :] = (acc[u] + part_r[u].astype(F32)).astype(BF16)

    def kv_done(d, carry):
        kv_out(d).wait_send()
        forward(d).wait_send()
        dkv_out(2 * ((chip + d) % 8) + core).wait_send()
        m_copy(2 * ((chip + d) % 8) + 1 - core).wait_send()
        return carry

    lax.fori_loop(1, 8, kv_done, 0)
    to_sibling.wait_send()
    dkv_out(sibling).wait_send()
    pair_copy.wait_send()
    piece_copy.wait_send()
    weight_x.wait_send()
    pl.when(inner)(weight_on.wait_send)
    for u in range(2):
        c_copy(u).wait_send()
        for way in range(2):
            y_copy(u, way).wait_send()
            f_copy(u, way).wait_send()
        for i in range(5):
            s_copy(u, i, core).wait_send()
    for way in range(2):
        for k in range(1, 5):
            for u in range(2):
                if hops(way, k, u):
                    z_copy(way, k, u).wait_send()
                    p_copy(way, k, u).wait_send()


def local(queries, keys, values, grad_attn, segment_ids, q_weight):
    rows, width = queries.shape
    vmem = pl.BlockSpec(memory_space=pltpu.VMEM)
    anywhere = pl.BlockSpec(memory_space=pltpu.HBM)
    dma = pltpu.SemaphoreType.DMA
    scratch = [
        pltpu.VMEM((17, 2, HALF, HD), BF16),
        pltpu.VMEM((17, HALF, PER * HALF), F32),
        pltpu.VMEM((17, HALF, PER * HALF), F32),
        pltpu.VMEM((2, PER * HALF, HD), BF16),
        pltpu.VMEM((2, PER * HALF, HD), BF16),
        pltpu.VMEM((2, PER * HALF, HD), F32),
        pltpu.VMEM((8, 8, PER * HALF), F32),
        pltpu.VMEM((16, 2, HALF, HD), BF16),
        pltpu.VMEM((16, 2, HALF, HD), BF16),
        pltpu.VMEM((16, 2, HALF, HD), BF16),
        pltpu.VMEM((2, 2, HALF, HD), F32),
        pltpu.VMEM((2 * HALF, HD), BF16),
        pltpu.VMEM((2 * HALF, HD), BF16),
        pltpu.VMEM((8, 2 * HALF, PER * HD), BF16),
        pltpu.VMEM((8, 2, 2 * HALF, HD), BF16),
        pltpu.VMEM((8, 2, 512, 512), BF16),
        pltpu.VMEM((2, HALF, 512), F32),
        pltpu.VMEM((2, HALF, 512), BF16),
        pltpu.VMEM((2, HALF, 512), BF16),
    ]
    sizes = (4, 8, 8, 8, 8, 16, 16, 16, 16, 2, 2, 16, 16, 16, 16, 1, 2, 2, 4, 4, 4, 4, 10, 10, 2, 2)
    return pl.pallas_call(
        attention_kernel,
        out_shape=(
            jax.ShapeDtypeStruct((rows, width), BF16),
            jax.ShapeDtypeStruct((rows, KVH * HD), BF16),
            jax.ShapeDtypeStruct((rows, KVH * HD), BF16),
        ),
        in_specs=[vmem, anywhere, anywhere, vmem, vmem, anywhere],
        out_specs=(vmem, vmem, vmem),
        scratch_shapes=scratch + [dma((size,)) for size in sizes],
        compiler_params=pltpu.CompilerParams(
            collective_id=0, has_side_effects=True, vmem_limit_bytes=48 * 1024 * 1024
        ),
    )(queries, keys, values, grad_attn, segment_ids.reshape(32, 128), q_weight)


def solution(mesh):
    placed = (
        P("row", "col"),
        P("row", None),
        P("row", None),
        P("row", "col"),
        P(),
        P("row", "col"),
    )
    return jax.shard_map(
        local,
        mesh=mesh,
        in_specs=placed,
        out_specs=(P("row", "col"), P("row", None), P("row", None)),
        check_vma=False,
    )
```

```python
import functools
import math

import jax
import jax.numpy as jnp
from jax import lax
from jax.experimental import pallas as pl
from jax.experimental.pallas import tpu as pltpu
from jax.sharding import PartitionSpec as P

H = 64
KVH = 8
HD = 128
TOKENS = 4096
HALF = 128
PER = 4
NEG = -1e30
MESH = pl.DeviceIdType.MESH
INV_ROOT = 1.0 / math.sqrt(HD)
SCALE2 = INV_ROOT * math.log2(math.e)
F32 = jnp.float32
BF16 = jnp.bfloat16


def dot_nt(a, b):
    return lax.dot_general(a, b, (((1,), (1,)), ((), ())), preferred_element_type=F32)


def dot_nn(a, b):
    return lax.dot_general(a, b, (((1,), (0,)), ((), ())), preferred_element_type=F32)


def dot_tn(a, b):
    return lax.dot_general(a, b, (((0,), (0,)), ((), ())), preferred_element_type=F32)


def attention_kernel(
    q_hbm, k_hbm, v_hbm, g_hbm, seg_hbm, w_hbm,
    out_ref, kout_ref, vout_ref,
    kvbuf, sbuf, dpbuf, q4, g4, dq4, stat, pbuf, mbuf, rbuf, ownf, pair_s, pair_r, dqbuf, pieces,
    wbuf, acc, part_s, part_r, seg_ref,
    load_sem, q_sem, kv_send, kv_recv, fw_send, fw_recv, m_send, m_recv, dkv_send, dkv_recv, pair_sem,
    xp_sem, z_send, z_recv, p_send, p_recv,
    wl_sem, wx_send, wx_recv, wy_send, wy_recv, wf_send, wf_recv, ws_send, ws_recv, c_send, c_recv,
):
    s = lax.axis_index("row")
    j = lax.axis_index("col")
    chip, core = s // 2, s % 2
    xl, y = chip // 4, chip % 4
    xh, z = j // 8, j % 8
    sibling = s + 1 - 2 * core
    partner = (1 - xh) * 8 + z
    right = xh * 8 + (z + 1) % 8
    left = xh * 8 + (z + 7) % 8
    parity = z % 2
    mate = j + 1 - 2 * parity
    head = j // 2
    inner = xl != xh
    outer = xl == xh

    def remote(src, dst, ssem, rsem, row, col):
        return pltpu.make_async_remote_copy(
            src_ref=src, dst_ref=dst, send_sem=ssem, recv_sem=rsem,
            device_id=(row, col), device_id_type=MESH,
        )

    lanes = pl.ds(pl.multiple_of(head * HD, HD), HD)
    loads = []
    for u in range(2):
        slot = s if u == 0 else 16
        for i, ref in enumerate((k_hbm, v_hbm)):
            loads.append(
                pltpu.make_async_copy(
                    ref.at[pl.ds(u * HALF, HALF), lanes], kvbuf.at[slot, i], load_sem.at[2 * u + i]
                )
            )
    for copy in loads:
        copy.start()
    for u in range(2):
        for h in range(PER):
            for i, (ref, buf) in enumerate(((q_hbm, q4), (g_hbm, g4))):
                pltpu.make_async_copy(
                    ref.at[pl.ds(u * HALF, HALF), pl.ds(h * HD, HD)],
                    buf.at[u, pl.ds(h * HD, HD)],
                    q_sem.at[i],
                ).start()
    seg_load = pltpu.make_async_copy(seg_hbm, seg_ref, q_sem.at[2])
    seg_load.start()

    barrier = pltpu.get_barrier_semaphore()

    def greet(e, carry):
        pl.semaphore_signal(barrier, inc=1, device_id=((s + e) % 16, j), device_id_type=MESH)
        return carry

    lax.fori_loop(1, 16, greet, 0)
    across = (1 - xl) * 8 + y * 2 + core
    for row, col in ((s, right), (s, left), (s, partner), (across, partner)):
        pl.semaphore_signal(barrier, inc=1, device_id=(row, col), device_id_type=MESH)

    seg_load.wait()
    seg = seg_ref[...]
    counts = [jnp.sum((seg < v).astype(F32), keepdims=True) for v in (1, 2, 3)]
    lane = lax.broadcasted_iota(jnp.int32, (1, HALF), 1).astype(F32)
    bounds = []
    for u in range(2):
        block = s if u == 0 else 31 - s
        seg_q = seg_ref[pl.ds(block, 1), :]
        start = jnp.where(
            seg_q == 0, 0.0,
            jnp.where(seg_q == 1, counts[0], jnp.where(seg_q == 2, counts[1], counts[2])),
        )
        stat[4 + u, 0:1, 0:HALF] = start
        stat[4 + u, 1:2, 0:HALF] = lane + (block * HALF).astype(F32)
        stat[u] = jnp.full((8, PER * HALF), NEG, F32)

    for copy in loads:
        copy.wait()
    pltpu.make_async_copy(q4, q4, q_sem.at[0]).wait()
    pltpu.make_async_copy(g4, g4, q_sem.at[1]).wait()
    pl.semaphore_wait(barrier, 19)

    def kv_copy(d, chip_to, row_to):
        src = kvbuf.at[jnp.where(chip_to > chip, s, 16)]
        return remote(src, kvbuf.at[s], kv_send.at[d], kv_recv.at[d], row_to, j)

    def kv_out(d):
        chip_to = (chip + d) % 8
        return kv_copy(d, chip_to, chip_to * 2 + core)

    def kv_start(d, carry):
        kv_out(d).start()
        return carry

    own_half = kvbuf.at[jnp.where(core == 0, s, 16)]
    to_sibling = remote(own_half, kvbuf.at[s], kv_send.at[0], kv_recv.at[0], sibling, j)
    lax.fori_loop(1, 8, kv_start, 0)
    to_sibling.start()

    slot = 2 * y + core
    own_weight = pltpu.make_async_copy(w_hbm, wbuf.at[slot, xh], wl_sem.at[0])

    def quarter(i):
        return pl.ds(i * 128, 128)

    def x_copy(i):
        return remote(
            w_hbm.at[quarter(i)], wbuf.at[slot, xh, quarter(i)],
            wx_send.at[i], wx_recv.at[4 * xh + i], across, xl * 8 + z,
        )

    def on_copy(i):
        ref = wbuf.at[slot, 1 - xh, quarter(i)]
        return remote(ref, ref, wx_send.at[4 + i], wx_recv.at[4 * (1 - xh) + i], across, j)

    def slot_at(step, which):
        return 2 * ((y + step) % 4) + which

    def row_at(step):
        return xl * 8 + ((y + step) % 4) * 2 + core

    def x_wait(e, i):
        ref = wbuf.at[slot, e, quarter(i)]
        remote(ref, ref, wx_send.at[0], wx_recv.at[4 * e + i], across, j).wait_recv()

    def y_copy(e, way):
        ref = wbuf.at[slot, e]
        index = 2 * e + way
        return remote(ref, ref, wy_send.at[index], wy_recv.at[index], row_at(3 if way else 1), j)

    def y_wait(e, way):
        ref = wbuf.at[slot_at(1 if way else 3, core), e]
        index = 2 * e + way
        remote(ref, ref, wy_send.at[index], wy_recv.at[index], s, right).wait_recv()

    def f_ref(step, e, way):
        return wbuf.at[slot_at(step, core), e, pl.ds(way * 256, 256)]

    def f_copy(e, way):
        ref = f_ref(1 if way else 3, e, way)
        index = 2 * e + way
        return remote(ref, ref, wf_send.at[index], wf_recv.at[index], row_at(3 if way else 1), j)

    def f_wait(e, way):
        ref = f_ref(2, e, way)
        index = 2 * e + way
        remote(ref, ref, wf_send.at[index], wf_recv.at[index], s, right).wait_recv()

    def s_copy(e, i, which):
        if i < 3:
            ref = wbuf.at[slot_at((0, 3, 1)[i], which), e]
        else:
            ref = wbuf.at[slot_at(2, which), e, pl.ds((i - 3) * 256, 256)]
        index = 5 * e + i
        return remote(ref, ref, ws_send.at[index], ws_recv.at[index], sibling, j)

    def y_start(e, i, ref):
        for way in range(2):
            index = 2 * e + way
            remote(
                ref, wbuf.at[slot, e, quarter(i)], wy_send.at[index], wy_recv.at[index],
                row_at(3 if way else 1), j,
            ).start()

    for i in range(4):
        x_copy(i).start()

    @pl.when(outer)
    def _():
        own_weight.start()
        for i in range(4):
            y_start(xh, i, w_hbm.at[quarter(i)])

    def weight_inner(i):
        x_wait(1 - xh, i)
        on_copy(i).start()
        x_wait(xh, i)
        y_start(xh, i, wbuf.at[slot, xh, quarter(i)])
        y_start(1 - xh, i, wbuf.at[slot, 1 - xh, quarter(i)])

    def weight_outer(i):
        x_wait(1 - xh, i)
        y_start(1 - xh, i, wbuf.at[slot, 1 - xh, quarter(i)])

    def weight_pass(e):
        for way in range(2):
            y_wait(e, way)
            f_copy(e, way).start()
            s_copy(e, 1 + way, core).start()

    def weight_last(e):
        for way in range(2):
            f_wait(e, way)
            s_copy(e, 3 + way, core).start()

    def weight_ready(e):
        for i in range(5):
            s_copy(e, i, 1 - core).wait_recv()

    sub = lax.broadcasted_iota(jnp.int32, (HALF, HALF), 0).astype(F32)

    def pass_one(t):
        u = jnp.where(t > s, 1, 0)
        block = jnp.where(t > s, jnp.where(t == 16, 31 - s, 31 - t), t)
        key_place = sub + (block * HALF).astype(F32)
        start = stat[4 + u, 0:1, 0:HALF]
        place = stat[4 + u, 1:2, 0:HALF]
        bias = jnp.where((key_place >= start) & (key_place <= place), 0.0, NEG)
        scores = dot_nt(kvbuf[t, 0], q4[u])
        for h in range(PER):
            part = scores[:, h * HALF:(h + 1) * HALF] * SCALE2 + bias
            sbuf[t, :, h * HALF:(h + 1) * HALF] = part
            top = jnp.max(part.reshape(16, 8, HALF), axis=0)
            stat[u, :, h * HALF:(h + 1) * HALF] = jnp.maximum(
                stat[u, :, h * HALF:(h + 1) * HALF], top
            )
        dpbuf[t] = dot_nt(kvbuf[t, 1], g4[u])

    pass_one(s)
    pass_one(16)

    def forward(d):
        origin = ((chip + 8 - d) % 8) * 2 + core
        return remote(kvbuf.at[origin], kvbuf.at[origin], fw_send.at[d], fw_recv.at[d], sibling, j)

    def arrive(d, carry):
        origin = ((chip + 8 - d) % 8) * 2 + core
        remote(
            kvbuf.at[origin], kvbuf.at[origin], kv_send.at[d], kv_recv.at[d], sibling, j
        ).wait_recv()
        forward(d).start()
        pass_one(origin)
        return carry

    lax.fori_loop(1, 8, arrive, 0)

    @pl.when(inner)
    def _():
        weight_inner(0)
        weight_inner(1)

    remote(
        kvbuf.at[sibling], kvbuf.at[sibling], kv_send.at[0], kv_recv.at[0], sibling, j
    ).wait_recv()
    pass_one(sibling)

    def arrive_two(d, carry):
        origin = ((chip + 8 - d) % 8) * 2 + 1 - core
        remote(
            kvbuf.at[origin], kvbuf.at[origin], fw_send.at[d], fw_recv.at[d], sibling, j
        ).wait_recv()
        pass_one(origin)
        return carry

    lax.fori_loop(1, 8, arrive_two, 0)

    @pl.when(inner)
    def _():
        weight_inner(2)
        weight_inner(3)

    for u in range(2):
        top = jnp.max(stat[u], axis=0, keepdims=True)
        stat[u] = jnp.broadcast_to(top, (8, PER * HALF))
        stat[2 + u] = jnp.zeros((8, PER * HALF), F32)
        stat[6 + u] = jnp.zeros((8, PER * HALF), F32)

    def pass_two(t, carry):
        u = jnp.where(t > s, 1, 0)
        for h in range(PER):
            cols = slice(h * HALF, (h + 1) * HALF)
            top = stat[u, 0:1, cols]
            expo = jnp.exp2(sbuf[t, :, cols] - top)
            sbuf[t, :, cols] = expo
            stat[2 + u, :, cols] += jnp.sum(expo.reshape(16, 8, HALF), axis=0)
            stat[6 + u, :, cols] += jnp.sum((expo * dpbuf[t, :, cols]).reshape(16, 8, HALF), axis=0)
        return carry

    lax.fori_loop(0, 17, pass_two, 0)

    @pl.when(outer)
    def _():
        own_weight.wait()
        for i in range(4):
            weight_outer(i)

    for e in range(2):
        s_copy(e, 0, core).start()

    for u in range(2):
        total = jnp.sum(stat[2 + u], axis=0, keepdims=True)
        inverse = 1.0 / total
        delta = jnp.sum(stat[6 + u], axis=0, keepdims=True) * inverse
        stat[2 + u, 0:1, :] = inverse
        stat[6 + u, 0:1, :] = delta
        dq4[u] = jnp.zeros((PER * HALF, HD), F32)

    def m_copy(t):
        return remote(pbuf.at[t], mbuf.at[t], m_send.at[t], m_recv.at[t], sibling, j)

    def dkv_out(t):
        return remote(pbuf.at[t], rbuf.at[s], dkv_send.at[t], dkv_recv.at[s], t, j)

    def pass_three(t, carry):
        u = jnp.where(t > s, 1, 0)
        inverse = stat[2 + u, 0:1, :]
        delta = stat[6 + u, 0:1, :]
        probs = sbuf[t] * inverse
        dscore = (probs * (dpbuf[t] - delta)).astype(BF16)
        key_part = dot_nn(dscore, q4[u])
        value_part = dot_nn(probs.astype(BF16), g4[u])
        dq4[u] += dot_tn(dscore, kvbuf[t, 0])
        mine = (t == s) | (t == 16)

        @pl.when(mine)
        def _():
            ownf[u, 0] = key_part
            ownf[u, 1] = value_part

        @pl.when(jnp.logical_not(mine))
        def _():
            pbuf[t, 0] = key_part.astype(BF16)
            pbuf[t, 1] = value_part.astype(BF16)

            @pl.when(t == sibling)
            def _():
                dkv_out(t).start()

            @pl.when((t != sibling) & (t % 2 != core))
            def _():
                m_copy(t).start()

        return carry

    def z_copy(way, k, u):
        origin = (z + 8 - (k - 1)) % 8 if way == 0 else (z + (k - 1)) % 8
        src = dqbuf.at[origin, pl.ds(u * HALF, HALF)]
        index = (way * 4 + (k - 1)) * 2 + u
        return remote(src, src, z_send.at[index], z_recv.at[index], s, right if way == 0 else left)

    def z_wait(way, k, u):
        origin = (z + 8 - k) % 8 if way == 0 else (z + k) % 8
        dst = dqbuf.at[origin, pl.ds(u * HALF, HALF)]
        index = (way * 4 + (k - 1)) * 2 + u
        remote(dst, dst, z_send.at[index], z_recv.at[index], s, right).wait_recv()

    def hops(way, k, u):
        return k <= 3 or u == way

    def z_turn(k):
        for u in (1, 0):
            for way in range(2):
                if hops(way, k, u):
                    z_wait(way, k, u)
                    if k < 4 and hops(way, k + 1, u):
                        z_copy(way, k + 1, u).start()

    for u, first, last in ((1, s + 1, 17), (0, 0, s + 1)):
        lax.fori_loop(first, last, pass_three, 0)
        for h in range(PER):
            dqbuf[z, u * HALF:(u + 1) * HALF, h * HD:(h + 1) * HD] = (
                dq4[u, h * HD:(h + 1) * HD, :] * INV_ROOT
            ).astype(BF16)
        z_copy(0, 1, u).start()
        z_copy(1, 1, u).start()

    def merge(d, carry):
        t = 2 * ((chip + d) % 8) + core
        remote(pbuf.at[t], mbuf.at[t], m_send.at[t], m_recv.at[t], sibling, j).wait_recv()
        for i in range(2):
            pbuf[t, i] = (pbuf[t, i].astype(F32) + mbuf[t, i].astype(F32)).astype(BF16)
        dkv_out(t).start()
        return carry

    lax.fori_loop(1, 8, merge, 0)
    weight_pass(xh)
    z_turn(1)
    z_turn(2)

    def dkv_take(r):
        remote(rbuf.at[r], rbuf.at[r], dkv_send.at[r], dkv_recv.at[r], s, right).wait_recv()
        u = jnp.where(r > s, 0, 1)
        for i in range(2):
            ownf[u, i] += rbuf[r, i].astype(F32)

    def take(d, carry):
        dkv_take(2 * ((chip + 8 - d) % 8) + core)
        return carry

    dkv_take(sibling)
    lax.fori_loop(1, 8, take, 0)
    for u in range(2):
        pair_s[u * HALF:(u + 1) * HALF, :] = ownf[u, 1 - parity].astype(BF16)
    pair_copy = remote(pair_s, pair_r, pair_sem.at[0], pair_sem.at[1], s, mate)
    pair_copy.start()

    z_turn(3)
    weight_pass(1 - xh)

    pair_copy.wait_recv()
    factor = jnp.where(parity == 0, INV_ROOT, 1.0).astype(F32)
    for u in range(2):
        rows = slice(u * HALF, (u + 1) * HALF)
        pieces[z, xh, rows, :] = (
            (ownf[u, parity] + pair_r[rows, :].astype(F32)) * factor
        ).astype(BF16)
    piece = pieces.at[z, xh]
    piece_copy = remote(piece, piece, xp_sem.at[0], xp_sem.at[1], s, partner)
    piece_copy.start()

    z_turn(4)
    other = pieces.at[z, 1 - xh]
    remote(other, other, xp_sem.at[0], xp_sem.at[1], s, partner).wait_recv()

    def p_copy(way, k, i):
        origin = (z + 8 - (k - 1)) % 8 if way == 0 else (z + (k - 1)) % 8
        src = pieces.at[origin, i]
        index = (way * 4 + (k - 1)) * 2 + i
        return remote(src, src, p_send.at[index], p_recv.at[index], s, right if way == 0 else left)

    def p_wait(way, k, i):
        origin = (z + 8 - k) % 8 if way == 0 else (z + k) % 8
        dst = pieces.at[origin, i]
        index = (way * 4 + (k - 1)) * 2 + i
        remote(dst, dst, p_send.at[index], p_recv.at[index], s, right).wait_recv()

    for i in range(2):
        p_copy(0, 1, i).start()
        p_copy(1, 1, i).start()

    def p_turn(k):
        for i in (1, 0):
            for way in range(2):
                if hops(way, k, i):
                    p_wait(way, k, i)
                    if k < 4 and hops(way, k + 1, i):
                        p_copy(way, k + 1, i).start()

    def product(e):
        acc[...] = jnp.zeros((2 * HALF, 512), F32)

        def add(zz, carry):
            acc[...] += dot_nn(dqbuf[zz], wbuf[zz, e])
            return carry

        lax.fori_loop(0, 8, add, 0)

    def c_copy(u):
        return remote(part_s.at[u], part_r.at[u], c_send.at[u], c_recv.at[u], s, partner)

    weight_last(1 - xh)
    weight_ready(1 - xh)
    product(1 - xh)
    for u in range(2):
        part_s[u] = acc[u * HALF:(u + 1) * HALF, :].astype(BF16)
        c_copy(u).start()
    p_turn(1)
    weight_last(xh)
    p_turn(2)
    weight_ready(xh)
    product(xh)
    p_turn(3)
    p_turn(4)
    for g in range(KVH):
        cols = slice(g * HD, (g + 1) * HD)
        kout_ref[:, cols] = pieces[2 * (g % 4), g // 4]
        vout_ref[:, cols] = pieces[2 * (g % 4) + 1, g // 4]

    for u in range(2):
        c_copy(u).wait_recv()
        rows = slice(u * HALF, (u + 1) * HALF)
        out_ref[rows, :] = (acc[rows, :] + part_r[u].astype(F32)).astype(BF16)

    def kv_done(d, carry):
        kv_out(d).wait_send()
        forward(d).wait_send()
        dkv_out(2 * ((chip + d) % 8) + core).wait_send()
        m_copy(2 * ((chip + d) % 8) + 1 - core).wait_send()
        return carry

    lax.fori_loop(1, 8, kv_done, 0)
    to_sibling.wait_send()
    dkv_out(sibling).wait_send()
    pair_copy.wait_send()
    piece_copy.wait_send()
    for i in range(4):
        x_copy(i).wait_send()

    @pl.when(inner)
    def _():
        for i in range(4):
            on_copy(i).wait_send()

    for u in range(2):
        c_copy(u).wait_send()
        for way in range(2):
            y_copy(u, way).wait_send()
            f_copy(u, way).wait_send()
        for i in range(5):
            s_copy(u, i, core).wait_send()
    for way in range(2):
        for k in range(1, 5):
            for u in range(2):
                if hops(way, k, u):
                    z_copy(way, k, u).wait_send()
                    p_copy(way, k, u).wait_send()


def local(queries, keys, values, grad_attn, segment_ids, q_weight):
    rows, width = queries.shape
    vmem = pl.BlockSpec(memory_space=pltpu.VMEM)
    anywhere = pl.BlockSpec(memory_space=pltpu.HBM)
    dma = pltpu.SemaphoreType.DMA
    scratch = [
        pltpu.VMEM((17, 2, HALF, HD), BF16),
        pltpu.VMEM((17, HALF, PER * HALF), F32),
        pltpu.VMEM((17, HALF, PER * HALF), F32),
        pltpu.VMEM((2, PER * HALF, HD), BF16),
        pltpu.VMEM((2, PER * HALF, HD), BF16),
        pltpu.VMEM((2, PER * HALF, HD), F32),
        pltpu.VMEM((8, 8, PER * HALF), F32),
        pltpu.VMEM((16, 2, HALF, HD), BF16),
        pltpu.VMEM((16, 2, HALF, HD), BF16),
        pltpu.VMEM((16, 2, HALF, HD), BF16),
        pltpu.VMEM((2, 2, HALF, HD), F32),
        pltpu.VMEM((2 * HALF, HD), BF16),
        pltpu.VMEM((2 * HALF, HD), BF16),
        pltpu.VMEM((8, 2 * HALF, PER * HD), BF16),
        pltpu.VMEM((8, 2, 2 * HALF, HD), BF16),
        pltpu.VMEM((8, 2, 512, 512), BF16),
        pltpu.VMEM((2 * HALF, 512), F32),
        pltpu.VMEM((2, HALF, 512), BF16),
        pltpu.VMEM((2, HALF, 512), BF16),
        pltpu.VMEM((32, 128), jnp.int32),
    ]
    sizes = (4, 3, 8, 8, 8, 8, 16, 16, 16, 16, 2, 2, 16, 16, 16, 16, 1, 8, 8, 4, 4, 4, 4, 10, 10, 2, 2)
    return pl.pallas_call(
        attention_kernel,
        out_shape=(
            jax.ShapeDtypeStruct((rows, width), BF16),
            jax.ShapeDtypeStruct((rows, KVH * HD), BF16),
            jax.ShapeDtypeStruct((rows, KVH * HD), BF16),
        ),
        in_specs=[anywhere] * 6,
        out_specs=(vmem, vmem, vmem),
        scratch_shapes=scratch + [dma((size,)) for size in sizes],
        compiler_params=pltpu.CompilerParams(
            collective_id=0, has_side_effects=True, vmem_limit_bytes=63 * 1024 * 1024
        ),
    )(queries, keys, values, grad_attn, segment_ids.reshape(32, 128), q_weight)


def solution(mesh):
    placed = (
        P("row", "col"),
        P("row", None),
        P("row", None),
        P("row", "col"),
        P(),
        P("row", "col"),
    )
    return jax.shard_map(
        local,
        mesh=mesh,
        in_specs=placed,
        out_specs=(P("row", "col"), P("row", None), P("row", None)),
        check_vma=False,
    )
```

```python
import functools
import math

import jax
import jax.numpy as jnp
from jax import lax
from jax.experimental import pallas as pl
from jax.experimental.pallas import tpu as pltpu
from jax.sharding import PartitionSpec as P

H = 64
KVH = 8
HD = 128
TOKENS = 4096
HALF = 128
PER = 4
NEG = -1e30
PLAN = (
    ("x0", "x1", "x2", "x3",),
    ("a",),
    (),
    ("i0", "i1",),
    ("i2",),
    ("m", "z1", "i3", "o", "b", "Wa", "z2", "d", "z3", "q", "Wb", "z4", "px", "La", "p1", "R1b", "P1b", "Lb", "p2", "R1a", "P1a", "R2a", "P2a", "p3", "R2b", "P2b", "p4",),
)
MESH = pl.DeviceIdType.MESH
INV_ROOT = 1.0 / math.sqrt(HD)
SCALE2 = INV_ROOT * math.log2(math.e)
F32 = jnp.float32
BF16 = jnp.bfloat16


def dot_nt(a, b):
    return lax.dot_general(a, b, (((1,), (1,)), ((), ())), preferred_element_type=F32)


def dot_nn(a, b):
    return lax.dot_general(a, b, (((1,), (0,)), ((), ())), preferred_element_type=F32)


def dot_tn(a, b):
    return lax.dot_general(a, b, (((0,), (0,)), ((), ())), preferred_element_type=F32)


def attention_kernel(
    q_hbm, k_hbm, v_hbm, g_hbm, seg_hbm, w_hbm,
    out_ref, kout_ref, vout_ref,
    kvbuf, sbuf, dpbuf, q4, g4, dq4, stat, pbuf, mbuf, rbuf, ownf, pair_s, pair_r, dqbuf, pieces,
    wbuf, acc, part_s, part_r, seg_ref,
    load_sem, q_sem, kv_send, kv_recv, fw_send, fw_recv, m_send, m_recv, dkv_send, dkv_recv, pair_sem,
    xp_sem, z_send, z_recv, p_send, p_recv,
    wl_sem, wx_send, wx_recv, wy_send, wy_recv, wf_send, wf_recv, ws_send, ws_recv, c_send, c_recv,
):
    s = lax.axis_index("row")
    j = lax.axis_index("col")
    chip, core = s // 2, s % 2
    xl, y = chip // 4, chip % 4
    xh, z = j // 8, j % 8
    sibling = s + 1 - 2 * core
    partner = (1 - xh) * 8 + z
    right = xh * 8 + (z + 1) % 8
    left = xh * 8 + (z + 7) % 8
    parity = z % 2
    mate = j + 1 - 2 * parity
    head = j // 2
    inner = xl != xh
    outer = xl == xh

    def remote(src, dst, ssem, rsem, row, col):
        return pltpu.make_async_remote_copy(
            src_ref=src, dst_ref=dst, send_sem=ssem, recv_sem=rsem,
            device_id=(row, col), device_id_type=MESH,
        )

    lanes = pl.ds(pl.multiple_of(head * HD, HD), HD)
    loads = []
    for u in range(2):
        slot = s if u == 0 else 16
        for i, ref in enumerate((k_hbm, v_hbm)):
            loads.append(
                pltpu.make_async_copy(
                    ref.at[pl.ds(u * HALF, HALF), lanes], kvbuf.at[slot, i], load_sem.at[2 * u + i]
                )
            )
    for copy in loads:
        copy.start()
    for u in range(2):
        for h in range(PER):
            for i, (ref, buf) in enumerate(((q_hbm, q4), (g_hbm, g4))):
                pltpu.make_async_copy(
                    ref.at[pl.ds(u * HALF, HALF), pl.ds(h * HD, HD)],
                    buf.at[u, pl.ds(h * HD, HD)],
                    q_sem.at[i],
                ).start()
    seg_load = pltpu.make_async_copy(seg_hbm, seg_ref, q_sem.at[2])
    seg_load.start()

    barrier = pltpu.get_barrier_semaphore()

    def greet(e, carry):
        pl.semaphore_signal(barrier, inc=1, device_id=((s + e) % 16, j), device_id_type=MESH)
        return carry

    lax.fori_loop(1, 16, greet, 0)
    across = (1 - xl) * 8 + y * 2 + core
    for row, col in ((s, right), (s, left), (s, partner), (across, partner)):
        pl.semaphore_signal(barrier, inc=1, device_id=(row, col), device_id_type=MESH)

    seg_load.wait()
    seg = seg_ref[...]
    counts = [jnp.sum((seg < v).astype(F32), keepdims=True) for v in (1, 2, 3)]
    lane = lax.broadcasted_iota(jnp.int32, (1, HALF), 1).astype(F32)
    bounds = []
    for u in range(2):
        block = s if u == 0 else 31 - s
        seg_q = seg_ref[pl.ds(block, 1), :]
        start = jnp.where(
            seg_q == 0, 0.0,
            jnp.where(seg_q == 1, counts[0], jnp.where(seg_q == 2, counts[1], counts[2])),
        )
        stat[4 + u, 0:1, 0:HALF] = start
        stat[4 + u, 1:2, 0:HALF] = lane + (block * HALF).astype(F32)
        stat[u] = jnp.full((8, PER * HALF), NEG, F32)

    for copy in loads:
        copy.wait()
    pltpu.make_async_copy(q4, q4, q_sem.at[0]).wait()
    pltpu.make_async_copy(g4, g4, q_sem.at[1]).wait()
    pl.semaphore_wait(barrier, 19)

    def kv_copy(d, chip_to, row_to):
        src = kvbuf.at[jnp.where(chip_to > chip, s, 16)]
        return remote(src, kvbuf.at[s], kv_send.at[d], kv_recv.at[d], row_to, j)

    def kv_out(d):
        chip_to = (chip + d) % 8
        return kv_copy(d, chip_to, chip_to * 2 + core)

    def kv_start(d, carry):
        kv_out(d).start()
        return carry

    own_half = kvbuf.at[jnp.where(core == 0, s, 16)]
    to_sibling = remote(own_half, kvbuf.at[s], kv_send.at[0], kv_recv.at[0], sibling, j)
    lax.fori_loop(1, 8, kv_start, 0)
    to_sibling.start()

    slot = 2 * y + core
    own_weight = pltpu.make_async_copy(w_hbm, wbuf.at[slot, xh], wl_sem.at[0])

    def quarter(i):
        return pl.ds(i * 128, 128)

    def x_copy(i):
        return remote(
            w_hbm.at[quarter(i)], wbuf.at[slot, xh, quarter(i)],
            wx_send.at[i], wx_recv.at[4 * xh + i], across, xl * 8 + z,
        )

    def on_copy(i):
        ref = wbuf.at[slot, 1 - xh, quarter(i)]
        return remote(ref, ref, wx_send.at[4 + i], wx_recv.at[4 * (1 - xh) + i], across, j)

    def slot_at(step, which):
        return 2 * ((y + step) % 4) + which

    def row_at(step):
        return xl * 8 + ((y + step) % 4) * 2 + core

    def x_wait(e, i):
        ref = wbuf.at[slot, e, quarter(i)]
        remote(ref, ref, wx_send.at[0], wx_recv.at[4 * e + i], across, j).wait_recv()

    def y_copy(e, way):
        ref = wbuf.at[slot, e]
        index = 2 * e + way
        return remote(ref, ref, wy_send.at[index], wy_recv.at[index], row_at(3 if way else 1), j)

    def y_wait(e, way):
        ref = wbuf.at[slot_at(1 if way else 3, core), e]
        index = 2 * e + way
        remote(ref, ref, wy_send.at[index], wy_recv.at[index], s, right).wait_recv()

    def f_ref(step, e, way):
        return wbuf.at[slot_at(step, core), e, pl.ds(way * 256, 256)]

    def f_copy(e, way):
        ref = f_ref(1 if way else 3, e, way)
        index = 2 * e + way
        return remote(ref, ref, wf_send.at[index], wf_recv.at[index], row_at(3 if way else 1), j)

    def f_wait(e, way):
        ref = f_ref(2, e, way)
        index = 2 * e + way
        remote(ref, ref, wf_send.at[index], wf_recv.at[index], s, right).wait_recv()

    def s_copy(e, i, which):
        if i < 3:
            ref = wbuf.at[slot_at((0, 3, 1)[i], which), e]
        else:
            ref = wbuf.at[slot_at(2, which), e, pl.ds((i - 3) * 256, 256)]
        index = 5 * e + i
        return remote(ref, ref, ws_send.at[index], ws_recv.at[index], sibling, j)

    def y_start(e, i, ref):
        for way in range(2):
            index = 2 * e + way
            remote(
                ref, wbuf.at[slot, e, quarter(i)], wy_send.at[index], wy_recv.at[index],
                row_at(3 if way else 1), j,
            ).start()

    steps = {}

    def run(stage):
        for name in PLAN[stage]:
            steps[name]()

    def send_own():
        @pl.when(outer)
        def _():
            own_weight.start()
            for i in range(4):
                y_start(xh, i, w_hbm.at[quarter(i)])

    def weight_inner(i):
        @pl.when(inner)
        def _():
            x_wait(1 - xh, i)
            on_copy(i).start()
            x_wait(xh, i)
            y_start(xh, i, wbuf.at[slot, xh, quarter(i)])
            if i == 3:
                s_copy(xh, 0, core).start()

    def weight_outer():
        @pl.when(outer)
        def _():
            own_weight.wait()
            s_copy(xh, 0, core).start()
            for i in range(4):
                x_wait(1 - xh, i)

    def send_other():
        y_copy(1 - xh, 0).start()
        y_copy(1 - xh, 1).start()
        s_copy(1 - xh, 0, core).start()

    for i in range(4):
        steps["x%d" % i] = x_copy(i).start
        steps["i%d" % i] = functools.partial(weight_inner, i)
    steps["a"] = send_own
    steps["o"] = weight_outer
    steps["b"] = send_other

    def weight_pass(e):
        for way in range(2):
            y_wait(e, way)
            f_copy(e, way).start()
            s_copy(e, 1 + way, core).start()

    def weight_last(e):
        for way in range(2):
            f_wait(e, way)
            s_copy(e, 3 + way, core).start()

    def weight_ready(e, first, last):
        for i in range(first, last):
            s_copy(e, i, 1 - core).wait_recv()

    for name, e in (("a", xh), ("b", 1 - xh)):
        steps["W" + name] = functools.partial(weight_pass, e)
        steps["L" + name] = functools.partial(weight_last, e)
        steps["R1" + name] = functools.partial(weight_ready, e, 0, 3)
        steps["R2" + name] = functools.partial(weight_ready, e, 3, 5)
    run(0)

    sub = lax.broadcasted_iota(jnp.int32, (HALF, HALF), 0).astype(F32)

    def pass_one(t):
        u = jnp.where(t > s, 1, 0)
        block = jnp.where(t > s, jnp.where(t == 16, 31 - s, 31 - t), t)
        key_place = sub + (block * HALF).astype(F32)
        start = stat[4 + u, 0:1, 0:HALF]
        place = stat[4 + u, 1:2, 0:HALF]
        bias = jnp.where((key_place >= start) & (key_place <= place), 0.0, NEG)
        scores = dot_nt(kvbuf[t, 0], q4[u])
        for h in range(PER):
            part = scores[:, h * HALF:(h + 1) * HALF] * SCALE2 + bias
            sbuf[t, :, h * HALF:(h + 1) * HALF] = part
            top = jnp.max(part.reshape(16, 8, HALF), axis=0)
            stat[u, :, h * HALF:(h + 1) * HALF] = jnp.maximum(
                stat[u, :, h * HALF:(h + 1) * HALF], top
            )
        dpbuf[t] = dot_nt(kvbuf[t, 1], g4[u])

    pass_one(s)
    pass_one(16)

    def forward(d):
        origin = ((chip + 8 - d) % 8) * 2 + core
        return remote(kvbuf.at[origin], kvbuf.at[origin], fw_send.at[d], fw_recv.at[d], sibling, j)

    def arrive(d, carry):
        origin = ((chip + 8 - d) % 8) * 2 + core
        remote(
            kvbuf.at[origin], kvbuf.at[origin], kv_send.at[d], kv_recv.at[d], sibling, j
        ).wait_recv()
        forward(d).start()
        pass_one(origin)
        return carry

    lax.fori_loop(1, 8, arrive, 0)

    run(1)
    remote(
        kvbuf.at[sibling], kvbuf.at[sibling], kv_send.at[0], kv_recv.at[0], sibling, j
    ).wait_recv()
    pass_one(sibling)

    def arrive_two(d, carry):
        origin = ((chip + 8 - d) % 8) * 2 + 1 - core
        remote(
            kvbuf.at[origin], kvbuf.at[origin], fw_send.at[d], fw_recv.at[d], sibling, j
        ).wait_recv()
        pass_one(origin)
        return carry

    lax.fori_loop(1, 8, arrive_two, 0)

    run(2)

    for u in range(2):
        top = jnp.max(stat[u], axis=0, keepdims=True)
        stat[u] = jnp.broadcast_to(top, (8, PER * HALF))
        stat[2 + u] = jnp.zeros((8, PER * HALF), F32)
        stat[6 + u] = jnp.zeros((8, PER * HALF), F32)

    def pass_two(t, carry):
        u = jnp.where(t > s, 1, 0)
        for h in range(PER):
            cols = slice(h * HALF, (h + 1) * HALF)
            top = stat[u, 0:1, cols]
            expo = jnp.exp2(sbuf[t, :, cols] - top)
            sbuf[t, :, cols] = expo
            stat[2 + u, :, cols] += jnp.sum(expo.reshape(16, 8, HALF), axis=0)
            stat[6 + u, :, cols] += jnp.sum((expo * dpbuf[t, :, cols]).reshape(16, 8, HALF), axis=0)
        return carry

    lax.fori_loop(0, 17, pass_two, 0)

    run(3)
    for u in range(2):
        total = jnp.sum(stat[2 + u], axis=0, keepdims=True)
        inverse = 1.0 / total
        delta = jnp.sum(stat[6 + u], axis=0, keepdims=True) * inverse
        stat[2 + u, 0:1, :] = inverse
        stat[6 + u, 0:1, :] = delta
        dq4[u] = jnp.zeros((PER * HALF, HD), F32)

    def m_copy(t):
        return remote(pbuf.at[t], mbuf.at[t], m_send.at[t], m_recv.at[t], sibling, j)

    def dkv_out(t):
        return remote(pbuf.at[t], rbuf.at[s], dkv_send.at[t], dkv_recv.at[s], t, j)

    def pass_three(t, carry):
        u = jnp.where(t > s, 1, 0)
        inverse = stat[2 + u, 0:1, :]
        delta = stat[6 + u, 0:1, :]
        probs = sbuf[t] * inverse
        dscore = (probs * (dpbuf[t] - delta)).astype(BF16)
        key_part = dot_nn(dscore, q4[u])
        value_part = dot_nn(probs.astype(BF16), g4[u])
        dq4[u] += dot_tn(dscore, kvbuf[t, 0])
        mine = (t == s) | (t == 16)

        @pl.when(mine)
        def _():
            ownf[u, 0] = key_part
            ownf[u, 1] = value_part

        @pl.when(jnp.logical_not(mine))
        def _():
            pbuf[t, 0] = key_part.astype(BF16)
            pbuf[t, 1] = value_part.astype(BF16)

            @pl.when(t == sibling)
            def _():
                dkv_out(t).start()

            @pl.when((t != sibling) & (t % 2 != core))
            def _():
                m_copy(t).start()

        return carry

    def z_copy(way, k, u):
        origin = (z + 8 - (k - 1)) % 8 if way == 0 else (z + (k - 1)) % 8
        src = dqbuf.at[origin, pl.ds(u * HALF, HALF)]
        index = (way * 4 + (k - 1)) * 2 + u
        return remote(src, src, z_send.at[index], z_recv.at[index], s, right if way == 0 else left)

    def z_wait(way, k, u):
        origin = (z + 8 - k) % 8 if way == 0 else (z + k) % 8
        dst = dqbuf.at[origin, pl.ds(u * HALF, HALF)]
        index = (way * 4 + (k - 1)) * 2 + u
        remote(dst, dst, z_send.at[index], z_recv.at[index], s, right).wait_recv()

    def hops(way, k, u):
        return k <= 3 or u == way

    def z_turn(k):
        for u in (1, 0):
            for way in range(2):
                if hops(way, k, u):
                    z_wait(way, k, u)
                    if k < 4 and hops(way, k + 1, u):
                        z_copy(way, k + 1, u).start()

    for u, first, last in ((1, s + 1, 17), (0, 0, s + 1)):
        lax.fori_loop(first, last, pass_three, 0)
        for h in range(PER):
            dqbuf[z, u * HALF:(u + 1) * HALF, h * HD:(h + 1) * HD] = (
                dq4[u, h * HD:(h + 1) * HD, :] * INV_ROOT
            ).astype(BF16)
        z_copy(0, 1, u).start()
        z_copy(1, 1, u).start()
        if u == 1:
            run(4)

    def merge(d, carry):
        t = 2 * ((chip + d) % 8) + core
        remote(pbuf.at[t], mbuf.at[t], m_send.at[t], m_recv.at[t], sibling, j).wait_recv()
        for i in range(2):
            pbuf[t, i] = (pbuf[t, i].astype(F32) + mbuf[t, i].astype(F32)).astype(BF16)
        dkv_out(t).start()
        return carry

    steps["m"] = lambda: lax.fori_loop(1, 8, merge, 0)
    for k in range(1, 5):
        steps["z%d" % k] = functools.partial(z_turn, k)

    def dkv_take(r):
        remote(rbuf.at[r], rbuf.at[r], dkv_send.at[r], dkv_recv.at[r], s, right).wait_recv()
        u = jnp.where(r > s, 0, 1)
        for i in range(2):
            ownf[u, i] += rbuf[r, i].astype(F32)

    def take(d, carry):
        dkv_take(2 * ((chip + 8 - d) % 8) + core)
        return carry

    pair_copy = remote(pair_s, pair_r, pair_sem.at[0], pair_sem.at[1], s, mate)
    piece = pieces.at[z, xh]
    piece_copy = remote(piece, piece, xp_sem.at[0], xp_sem.at[1], s, partner)

    def gather_rows():
        dkv_take(sibling)
        lax.fori_loop(1, 8, take, 0)
        for u in range(2):
            pair_s[u * HALF:(u + 1) * HALF, :] = ownf[u, 1 - parity].astype(BF16)
        pair_copy.start()

    def make_piece():
        pair_copy.wait_recv()
        factor = jnp.where(parity == 0, INV_ROOT, 1.0).astype(F32)
        for u in range(2):
            rows = slice(u * HALF, (u + 1) * HALF)
            pieces[z, xh, rows, :] = (
                (ownf[u, parity] + pair_r[rows, :].astype(F32)) * factor
            ).astype(BF16)
        piece_copy.start()

    def p_copy(way, k, i):
        origin = (z + 8 - (k - 1)) % 8 if way == 0 else (z + (k - 1)) % 8
        src = pieces.at[origin, i]
        index = (way * 4 + (k - 1)) * 2 + i
        return remote(src, src, p_send.at[index], p_recv.at[index], s, right if way == 0 else left)

    def p_wait(way, k, i):
        origin = (z + 8 - k) % 8 if way == 0 else (z + k) % 8
        dst = pieces.at[origin, i]
        index = (way * 4 + (k - 1)) * 2 + i
        remote(dst, dst, p_send.at[index], p_recv.at[index], s, right).wait_recv()

    def p_begin():
        other = pieces.at[z, 1 - xh]
        remote(other, other, xp_sem.at[0], xp_sem.at[1], s, partner).wait_recv()
        for i in range(2):
            p_copy(0, 1, i).start()
            p_copy(1, 1, i).start()

    def p_turn(k):
        for i in (1, 0):
            for way in range(2):
                if hops(way, k, i):
                    p_wait(way, k, i)
                    if k < 4 and hops(way, k + 1, i):
                        p_copy(way, k + 1, i).start()

    def product(e, i, near):
        if near:
            acc[i] = jnp.zeros((2 * HALF, 512), F32)

        def add(n, carry):
            step = n // 2 + n // 4 if near else 2
            zz = 2 * ((y + step) % 4) + n % 2
            acc[i] += dot_nn(dqbuf[zz], wbuf[zz, e])
            return carry

        lax.fori_loop(0, 6 if near else 2, add, 0)

    def c_copy(u):
        return remote(part_s.at[u], part_r.at[u], c_send.at[u], c_recv.at[u], s, partner)

    def product_other():
        product(1 - xh, 1, False)
        for u in range(2):
            part_s[u] = acc[1, u * HALF:(u + 1) * HALF, :].astype(BF16)
            c_copy(u).start()

    steps["d"] = gather_rows
    steps["q"] = make_piece
    steps["px"] = p_begin
    for k in range(1, 5):
        steps["p%d" % k] = functools.partial(p_turn, k)
    steps["P1a"] = functools.partial(product, xh, 0, True)
    steps["P2a"] = functools.partial(product, xh, 0, False)
    steps["P1b"] = functools.partial(product, 1 - xh, 1, True)
    steps["P2b"] = product_other
    run(5)
    for g in range(KVH):
        cols = slice(g * HD, (g + 1) * HD)
        kout_ref[:, cols] = pieces[2 * (g % 4), g // 4]
        vout_ref[:, cols] = pieces[2 * (g % 4) + 1, g // 4]

    for u in range(2):
        c_copy(u).wait_recv()
        rows = slice(u * HALF, (u + 1) * HALF)
        out_ref[rows, :] = (acc[0, rows, :] + part_r[u].astype(F32)).astype(BF16)

    def kv_done(d, carry):
        kv_out(d).wait_send()
        forward(d).wait_send()
        dkv_out(2 * ((chip + d) % 8) + core).wait_send()
        m_copy(2 * ((chip + d) % 8) + 1 - core).wait_send()
        return carry

    lax.fori_loop(1, 8, kv_done, 0)
    to_sibling.wait_send()
    dkv_out(sibling).wait_send()
    pair_copy.wait_send()
    piece_copy.wait_send()
    for i in range(4):
        x_copy(i).wait_send()

    @pl.when(inner)
    def _():
        for i in range(4):
            on_copy(i).wait_send()

    for u in range(2):
        c_copy(u).wait_send()
        for way in range(2):
            y_copy(u, way).wait_send()
            f_copy(u, way).wait_send()
        for i in range(5):
            s_copy(u, i, core).wait_send()
    for way in range(2):
        for k in range(1, 5):
            for u in range(2):
                if hops(way, k, u):
                    z_copy(way, k, u).wait_send()
                    p_copy(way, k, u).wait_send()


def local(queries, keys, values, grad_attn, segment_ids, q_weight):
    rows, width = queries.shape
    vmem = pl.BlockSpec(memory_space=pltpu.VMEM)
    anywhere = pl.BlockSpec(memory_space=pltpu.HBM)
    dma = pltpu.SemaphoreType.DMA
    scratch = [
        pltpu.VMEM((17, 2, HALF, HD), BF16),
        pltpu.VMEM((17, HALF, PER * HALF), F32),
        pltpu.VMEM((17, HALF, PER * HALF), F32),
        pltpu.VMEM((2, PER * HALF, HD), BF16),
        pltpu.VMEM((2, PER * HALF, HD), BF16),
        pltpu.VMEM((2, PER * HALF, HD), F32),
        pltpu.VMEM((8, 8, PER * HALF), F32),
        pltpu.VMEM((16, 2, HALF, HD), BF16),
        pltpu.VMEM((16, 2, HALF, HD), BF16),
        pltpu.VMEM((16, 2, HALF, HD), BF16),
        pltpu.VMEM((2, 2, HALF, HD), F32),
        pltpu.VMEM((2 * HALF, HD), BF16),
        pltpu.VMEM((2 * HALF, HD), BF16),
        pltpu.VMEM((8, 2 * HALF, PER * HD), BF16),
        pltpu.VMEM((8, 2, 2 * HALF, HD), BF16),
        pltpu.VMEM((8, 2, 512, 512), BF16),
        pltpu.VMEM((2, 2 * HALF, 512), F32),
        pltpu.VMEM((2, HALF, 512), BF16),
        pltpu.VMEM((2, HALF, 512), BF16),
        pltpu.VMEM((32, 128), jnp.int32),
    ]
    sizes = (4, 3, 8, 8, 8, 8, 16, 16, 16, 16, 2, 2, 16, 16, 16, 16, 1, 8, 8, 4, 4, 4, 4, 10, 10, 2, 2)
    return pl.pallas_call(
        attention_kernel,
        out_shape=(
            jax.ShapeDtypeStruct((rows, width), BF16),
            jax.ShapeDtypeStruct((rows, KVH * HD), BF16),
            jax.ShapeDtypeStruct((rows, KVH * HD), BF16),
        ),
        in_specs=[anywhere] * 6,
        out_specs=(vmem, vmem, vmem),
        scratch_shapes=scratch + [dma((size,)) for size in sizes],
        compiler_params=pltpu.CompilerParams(
            collective_id=0, has_side_effects=True, vmem_limit_bytes=63 * 1024 * 1024
        ),
    )(queries, keys, values, grad_attn, segment_ids.reshape(32, 128), q_weight)


def solution(mesh):
    placed = (
        P("row", "col"),
        P("row", None),
        P("row", None),
        P("row", "col"),
        P(),
        P("row", "col"),
    )
    return jax.shard_map(
        local,
        mesh=mesh,
        in_specs=placed,
        out_specs=(P("row", "col"), P("row", None), P("row", None)),
        check_vma=False,
    )
```

```python
import functools
import math

import jax
import jax.numpy as jnp
from jax import lax
from jax.experimental import pallas as pl
from jax.experimental.pallas import tpu as pltpu
from jax.sharding import PartitionSpec as P

H = 64
KVH = 8
HD = 128
TOKENS = 4096
HALF = 128
PER = 4
NEG = -1e30
PLAN = (
    ("x0",),
    ("a", "x1", "x2",),
    ("x3", "i0",),
    ("i1",),
    ("i2",),
    ("m", "z1", "i3", "o", "b", "Wa", "z2", "d", "z3", "q", "z4", "px", "Wb", "La", "p1", "R1b", "P1b", "Lb", "p2", "R1a", "P1a", "R2b", "P2b", "R2a", "P2a", "p3", "p4",),
)
MESH = pl.DeviceIdType.MESH
INV_ROOT = 1.0 / math.sqrt(HD)
SCALE2 = INV_ROOT * math.log2(math.e)
F32 = jnp.float32
BF16 = jnp.bfloat16


def dot_nt(a, b):
    return lax.dot_general(a, b, (((1,), (1,)), ((), ())), preferred_element_type=F32)


def dot_nn(a, b):
    return lax.dot_general(a, b, (((1,), (0,)), ((), ())), preferred_element_type=F32)


def dot_tn(a, b):
    return lax.dot_general(a, b, (((0,), (0,)), ((), ())), preferred_element_type=F32)


def attention_kernel(
    q_hbm, k_hbm, v_hbm, g_hbm, seg_hbm, w_hbm,
    own_hbm, part_hbm, kout_hbm, vout_hbm,
    kvbuf, sbuf, dpbuf, q4, g4, dq4, stat, pbuf, mbuf, rbuf, ownf, pair_s, pair_r, dqbuf, pieces,
    wbuf, acc, part_s, part_r, seg_ref,
    load_sem, q_sem, out_sem, kv_send, kv_recv, fw_send, fw_recv, m_send, m_recv, dkv_send, dkv_recv, pair_sem,
    xp_sem, z_send, z_recv, p_send, p_recv,
    wl_sem, wx_send, wx_recv, wy_send, wy_recv, wf_send, wf_recv, ws_send, ws_recv, c_send, c_recv,
):
    s = lax.axis_index("row")
    j = lax.axis_index("col")
    chip, core = s // 2, s % 2
    xl, y = chip // 4, chip % 4
    xh, z = j // 8, j % 8
    sibling = s + 1 - 2 * core
    partner = (1 - xh) * 8 + z
    right = xh * 8 + (z + 1) % 8
    left = xh * 8 + (z + 7) % 8
    parity = z % 2
    mate = j + 1 - 2 * parity
    head = j // 2
    inner = xl != xh
    outer = xl == xh

    def remote(src, dst, ssem, rsem, row, col):
        return pltpu.make_async_remote_copy(
            src_ref=src, dst_ref=dst, send_sem=ssem, recv_sem=rsem,
            device_id=(row, col), device_id_type=MESH,
        )

    lanes = pl.ds(pl.multiple_of(head * HD, HD), HD)
    loads = []
    for u in range(2):
        slot = s if u == 0 else 16
        for i, ref in enumerate((k_hbm, v_hbm)):
            loads.append(
                pltpu.make_async_copy(
                    ref.at[pl.ds(u * HALF, HALF), lanes], kvbuf.at[slot, i], load_sem.at[2 * u + i]
                )
            )
    for copy in loads:
        copy.start()
    for u in range(2):
        for h in range(PER):
            for i, (ref, buf) in enumerate(((q_hbm, q4), (g_hbm, g4))):
                pltpu.make_async_copy(
                    ref.at[pl.ds(u * HALF, HALF), pl.ds(h * HD, HD)],
                    buf.at[u, pl.ds(h * HD, HD)],
                    q_sem.at[i],
                ).start()
    seg_load = pltpu.make_async_copy(seg_hbm, seg_ref, q_sem.at[2])
    seg_load.start()

    barrier = pltpu.get_barrier_semaphore()

    def greet(e, carry):
        pl.semaphore_signal(barrier, inc=1, device_id=((s + e) % 16, j), device_id_type=MESH)
        return carry

    lax.fori_loop(1, 16, greet, 0)
    across = (1 - xl) * 8 + y * 2 + core
    for row, col in ((s, right), (s, left), (s, partner), (across, partner)):
        pl.semaphore_signal(barrier, inc=1, device_id=(row, col), device_id_type=MESH)

    seg_load.wait()
    seg = seg_ref[...]
    counts = [jnp.sum((seg < v).astype(F32), keepdims=True) for v in (1, 2, 3)]
    lane = lax.broadcasted_iota(jnp.int32, (1, HALF), 1).astype(F32)
    bounds = []
    for u in range(2):
        block = s if u == 0 else 31 - s
        seg_q = seg_ref[pl.ds(block, 1), :]
        start = jnp.where(
            seg_q == 0, 0.0,
            jnp.where(seg_q == 1, counts[0], jnp.where(seg_q == 2, counts[1], counts[2])),
        )
        stat[4 + u, 0:1, 0:HALF] = start
        stat[4 + u, 1:2, 0:HALF] = lane + (block * HALF).astype(F32)
        stat[u] = jnp.full((8, PER * HALF), NEG, F32)

    for copy in loads:
        copy.wait()
    pltpu.make_async_copy(q4, q4, q_sem.at[0]).wait()
    pltpu.make_async_copy(g4, g4, q_sem.at[1]).wait()
    pl.semaphore_wait(barrier, 19)

    def kv_copy(d, chip_to, row_to):
        src = kvbuf.at[jnp.where(chip_to > chip, s, 16)]
        return remote(src, kvbuf.at[s], kv_send.at[d], kv_recv.at[d], row_to, j)

    def kv_out(d):
        chip_to = (chip + d) % 8
        return kv_copy(d, chip_to, chip_to * 2 + core)

    def kv_start(d, carry):
        kv_out(d).start()
        return carry

    own_half = kvbuf.at[jnp.where(core == 0, s, 16)]
    to_sibling = remote(own_half, kvbuf.at[s], kv_send.at[0], kv_recv.at[0], sibling, j)
    lax.fori_loop(1, 8, kv_start, 0)
    to_sibling.start()

    slot = 2 * y + core
    own_weight = pltpu.make_async_copy(w_hbm, wbuf.at[slot, xh], wl_sem.at[0])

    def quarter(i):
        return pl.ds(i * 128, 128)

    def x_copy(i):
        return remote(
            w_hbm.at[quarter(i)], wbuf.at[slot, xh, quarter(i)],
            wx_send.at[i], wx_recv.at[4 * xh + i], across, xl * 8 + z,
        )

    def on_copy(i):
        ref = wbuf.at[slot, 1 - xh, quarter(i)]
        return remote(ref, ref, wx_send.at[4 + i], wx_recv.at[4 * (1 - xh) + i], across, j)

    def slot_at(step, which):
        return 2 * ((y + step) % 4) + which

    def row_at(step):
        return xl * 8 + ((y + step) % 4) * 2 + core

    def x_wait(e, i):
        ref = wbuf.at[slot, e, quarter(i)]
        remote(ref, ref, wx_send.at[0], wx_recv.at[4 * e + i], across, j).wait_recv()

    def y_copy(e, way):
        ref = wbuf.at[slot, e]
        index = 2 * e + way
        return remote(ref, ref, wy_send.at[index], wy_recv.at[index], row_at(3 if way else 1), j)

    def y_wait(e, way):
        ref = wbuf.at[slot_at(1 if way else 3, core), e]
        index = 2 * e + way
        remote(ref, ref, wy_send.at[index], wy_recv.at[index], s, right).wait_recv()

    def f_ref(step, e, way):
        return wbuf.at[slot_at(step, core), e, pl.ds(way * 256, 256)]

    def f_copy(e, way):
        ref = f_ref(1 if way else 3, e, way)
        index = 2 * e + way
        return remote(ref, ref, wf_send.at[index], wf_recv.at[index], row_at(3 if way else 1), j)

    def f_wait(e, way):
        ref = f_ref(2, e, way)
        index = 2 * e + way
        remote(ref, ref, wf_send.at[index], wf_recv.at[index], s, right).wait_recv()

    def s_copy(e, i, which):
        if i < 3:
            ref = wbuf.at[slot_at((0, 3, 1)[i], which), e]
        else:
            ref = wbuf.at[slot_at(2, which), e, pl.ds((i - 3) * 256, 256)]
        index = 5 * e + i
        return remote(ref, ref, ws_send.at[index], ws_recv.at[index], sibling, j)

    def y_start(e, i, ref):
        for way in range(2):
            index = 2 * e + way
            remote(
                ref, wbuf.at[slot, e, quarter(i)], wy_send.at[index], wy_recv.at[index],
                row_at(3 if way else 1), j,
            ).start()

    steps = {}

    def run(stage):
        for name in PLAN[stage]:
            steps[name]()

    def send_own():
        @pl.when(outer)
        def _():
            own_weight.start()
            for i in range(4):
                y_start(xh, i, w_hbm.at[quarter(i)])

    def weight_inner(i):
        @pl.when(inner)
        def _():
            x_wait(1 - xh, i)
            on_copy(i).start()
            x_wait(xh, i)
            y_start(xh, i, wbuf.at[slot, xh, quarter(i)])
            if i == 3:
                s_copy(xh, 0, core).start()

    def weight_outer():
        @pl.when(outer)
        def _():
            own_weight.wait()
            s_copy(xh, 0, core).start()
            for i in range(4):
                x_wait(1 - xh, i)

    def send_other():
        y_copy(1 - xh, 0).start()
        y_copy(1 - xh, 1).start()
        s_copy(1 - xh, 0, core).start()

    for i in range(4):
        steps["x%d" % i] = x_copy(i).start
        steps["i%d" % i] = functools.partial(weight_inner, i)
    steps["a"] = send_own
    steps["o"] = weight_outer
    steps["b"] = send_other

    def weight_pass(e):
        for way in range(2):
            y_wait(e, way)
            f_copy(e, way).start()
            s_copy(e, 1 + way, core).start()

    def weight_last(e):
        for way in range(2):
            f_wait(e, way)
            s_copy(e, 3 + way, core).start()

    def weight_ready(e, first, last):
        for i in range(first, last):
            s_copy(e, i, 1 - core).wait_recv()

    for name, e in (("a", xh), ("b", 1 - xh)):
        steps["W" + name] = functools.partial(weight_pass, e)
        steps["L" + name] = functools.partial(weight_last, e)
        steps["R1" + name] = functools.partial(weight_ready, e, 0, 3)
        steps["R2" + name] = functools.partial(weight_ready, e, 3, 5)
    run(0)

    sub = lax.broadcasted_iota(jnp.int32, (HALF, HALF), 0).astype(F32)

    def pass_one(t):
        u = jnp.where(t > s, 1, 0)
        block = jnp.where(t > s, jnp.where(t == 16, 31 - s, 31 - t), t)
        key_place = sub + (block * HALF).astype(F32)
        start = stat[4 + u, 0:1, 0:HALF]
        place = stat[4 + u, 1:2, 0:HALF]
        bias = jnp.where((key_place >= start) & (key_place <= place), 0.0, NEG)
        scores = dot_nt(kvbuf[t, 0], q4[u])
        for h in range(PER):
            part = scores[:, h * HALF:(h + 1) * HALF] * SCALE2 + bias
            sbuf[t, :, h * HALF:(h + 1) * HALF] = part
            top = jnp.max(part.reshape(16, 8, HALF), axis=0)
            stat[u, :, h * HALF:(h + 1) * HALF] = jnp.maximum(
                stat[u, :, h * HALF:(h + 1) * HALF], top
            )
        dpbuf[t] = dot_nt(kvbuf[t, 1], g4[u])

    pass_one(s)
    pass_one(16)

    def forward(d):
        origin = ((chip + 8 - d) % 8) * 2 + core
        return remote(kvbuf.at[origin], kvbuf.at[origin], fw_send.at[d], fw_recv.at[d], sibling, j)

    def arrive(d, carry):
        origin = ((chip + 8 - d) % 8) * 2 + core
        remote(
            kvbuf.at[origin], kvbuf.at[origin], kv_send.at[d], kv_recv.at[d], sibling, j
        ).wait_recv()
        forward(d).start()
        pass_one(origin)
        return carry

    lax.fori_loop(1, 8, arrive, 0)

    run(1)
    remote(
        kvbuf.at[sibling], kvbuf.at[sibling], kv_send.at[0], kv_recv.at[0], sibling, j
    ).wait_recv()
    pass_one(sibling)

    def arrive_two(d, carry):
        origin = ((chip + 8 - d) % 8) * 2 + 1 - core
        remote(
            kvbuf.at[origin], kvbuf.at[origin], fw_send.at[d], fw_recv.at[d], sibling, j
        ).wait_recv()
        pass_one(origin)
        return carry

    lax.fori_loop(1, 8, arrive_two, 0)

    run(2)

    for u in range(2):
        top = jnp.max(stat[u], axis=0, keepdims=True)
        stat[u] = jnp.broadcast_to(top, (8, PER * HALF))
        stat[2 + u] = jnp.zeros((8, PER * HALF), F32)
        stat[6 + u] = jnp.zeros((8, PER * HALF), F32)

    def pass_two(t, carry):
        u = jnp.where(t > s, 1, 0)
        for h in range(PER):
            cols = slice(h * HALF, (h + 1) * HALF)
            top = stat[u, 0:1, cols]
            expo = jnp.exp2(sbuf[t, :, cols] - top)
            sbuf[t, :, cols] = expo
            stat[2 + u, :, cols] += jnp.sum(expo.reshape(16, 8, HALF), axis=0)
            stat[6 + u, :, cols] += jnp.sum((expo * dpbuf[t, :, cols]).reshape(16, 8, HALF), axis=0)
        return carry

    lax.fori_loop(0, 17, pass_two, 0)

    run(3)
    for u in range(2):
        total = jnp.sum(stat[2 + u], axis=0, keepdims=True)
        inverse = 1.0 / total
        delta = jnp.sum(stat[6 + u], axis=0, keepdims=True) * inverse
        stat[2 + u, 0:1, :] = inverse
        stat[6 + u, 0:1, :] = delta
        dq4[u] = jnp.zeros((PER * HALF, HD), F32)

    def m_copy(t):
        return remote(pbuf.at[t], mbuf.at[t], m_send.at[t], m_recv.at[t], sibling, j)

    def dkv_out(t):
        return remote(pbuf.at[t], rbuf.at[s], dkv_send.at[t], dkv_recv.at[s], t, j)

    def pass_three(t, carry):
        u = jnp.where(t > s, 1, 0)
        inverse = stat[2 + u, 0:1, :]
        delta = stat[6 + u, 0:1, :]
        probs = sbuf[t] * inverse
        dscore = (probs * (dpbuf[t] - delta)).astype(BF16)
        key_part = dot_nn(dscore, q4[u])
        value_part = dot_nn(probs.astype(BF16), g4[u])
        dq4[u] += dot_tn(dscore, kvbuf[t, 0])
        mine = (t == s) | (t == 16)

        @pl.when(mine)
        def _():
            ownf[u, 0] = key_part
            ownf[u, 1] = value_part

        @pl.when(jnp.logical_not(mine))
        def _():
            pbuf[t, 0] = key_part.astype(BF16)
            pbuf[t, 1] = value_part.astype(BF16)

            @pl.when(t == sibling)
            def _():
                dkv_out(t).start()

            @pl.when((t != sibling) & (t % 2 != core))
            def _():
                m_copy(t).start()

        return carry

    def z_copy(way, k, u):
        origin = (z + 8 - (k - 1)) % 8 if way == 0 else (z + (k - 1)) % 8
        src = dqbuf.at[origin, pl.ds(u * HALF, HALF)]
        index = (way * 4 + (k - 1)) * 2 + u
        return remote(src, src, z_send.at[index], z_recv.at[index], s, right if way == 0 else left)

    def z_wait(way, k, u):
        origin = (z + 8 - k) % 8 if way == 0 else (z + k) % 8
        dst = dqbuf.at[origin, pl.ds(u * HALF, HALF)]
        index = (way * 4 + (k - 1)) * 2 + u
        remote(dst, dst, z_send.at[index], z_recv.at[index], s, right).wait_recv()

    def hops(way, k, u):
        return k <= 3 or u == way

    def z_turn(k):
        for u in (1, 0):
            for way in range(2):
                if hops(way, k, u):
                    z_wait(way, k, u)
                    if k < 4 and hops(way, k + 1, u):
                        z_copy(way, k + 1, u).start()

    for u, first, last in ((1, s + 1, 17), (0, 0, s + 1)):
        lax.fori_loop(first, last, pass_three, 0)
        for h in range(PER):
            dqbuf[z, u * HALF:(u + 1) * HALF, h * HD:(h + 1) * HD] = (
                dq4[u, h * HD:(h + 1) * HD, :] * INV_ROOT
            ).astype(BF16)
        z_copy(0, 1, u).start()
        z_copy(1, 1, u).start()
        if u == 1:
            run(4)

    def merge(d, carry):
        t = 2 * ((chip + d) % 8) + core
        remote(pbuf.at[t], mbuf.at[t], m_send.at[t], m_recv.at[t], sibling, j).wait_recv()
        for i in range(2):
            pbuf[t, i] = (pbuf[t, i].astype(F32) + mbuf[t, i].astype(F32)).astype(BF16)
        dkv_out(t).start()
        return carry

    steps["m"] = lambda: lax.fori_loop(1, 8, merge, 0)
    for k in range(1, 5):
        steps["z%d" % k] = functools.partial(z_turn, k)

    def dkv_take(r):
        remote(rbuf.at[r], rbuf.at[r], dkv_send.at[r], dkv_recv.at[r], s, right).wait_recv()
        u = jnp.where(r > s, 0, 1)
        for i in range(2):
            ownf[u, i] += rbuf[r, i].astype(F32)

    def take(d, carry):
        dkv_take(2 * ((chip + 8 - d) % 8) + core)
        return carry

    pair_copy = remote(pair_s, pair_r, pair_sem.at[0], pair_sem.at[1], s, mate)
    piece = pieces.at[z, xh]
    piece_copy = remote(piece, piece, xp_sem.at[0], xp_sem.at[1], s, partner)

    def gather_rows():
        dkv_take(sibling)
        lax.fori_loop(1, 8, take, 0)
        for u in range(2):
            pair_s[u * HALF:(u + 1) * HALF, :] = ownf[u, 1 - parity].astype(BF16)
        pair_copy.start()

    def make_piece():
        pair_copy.wait_recv()
        factor = jnp.where(parity == 0, INV_ROOT, 1.0).astype(F32)
        for u in range(2):
            rows = slice(u * HALF, (u + 1) * HALF)
            pieces[z, xh, rows, :] = (
                (ownf[u, parity] + pair_r[rows, :].astype(F32)) * factor
            ).astype(BF16)
        piece_copy.start()

    def p_copy(way, k, i):
        origin = (z + 8 - (k - 1)) % 8 if way == 0 else (z + (k - 1)) % 8
        src = pieces.at[origin, i]
        index = (way * 4 + (k - 1)) * 2 + i
        return remote(src, src, p_send.at[index], p_recv.at[index], s, right if way == 0 else left)

    def p_wait(way, k, i):
        origin = (z + 8 - k) % 8 if way == 0 else (z + k) % 8
        dst = pieces.at[origin, i]
        index = (way * 4 + (k - 1)) * 2 + i
        remote(dst, dst, p_send.at[index], p_recv.at[index], s, right).wait_recv()

    def p_begin():
        other = pieces.at[z, 1 - xh]
        remote(other, other, xp_sem.at[0], xp_sem.at[1], s, partner).wait_recv()
        for i in range(2):
            p_copy(0, 1, i).start()
            p_copy(1, 1, i).start()

    def p_turn(k):
        for i in (1, 0):
            for way in range(2):
                if hops(way, k, i):
                    p_wait(way, k, i)
                    if k < 4 and hops(way, k + 1, i):
                        p_copy(way, k + 1, i).start()

    def product(e, i, near):
        if near:
            acc[i] = jnp.zeros((2 * HALF, 512), F32)

        def add(n, carry):
            step = n // 2 + n // 4 if near else 2
            zz = 2 * ((y + step) % 4) + n % 2
            acc[i] += dot_nn(dqbuf[zz], wbuf[zz, e])
            return carry

        lax.fori_loop(0, 6 if near else 2, add, 0)

    def c_copy(u):
        return remote(part_s.at[u], part_r.at[u], c_send.at[u], c_recv.at[u], s, partner)

    def product_other():
        product(1 - xh, 1, False)
        for u in range(2):
            part_s[u] = acc[1, u * HALF:(u + 1) * HALF, :].astype(BF16)
            c_copy(u).start()

    steps["d"] = gather_rows
    steps["q"] = make_piece
    steps["px"] = p_begin
    for k in range(1, 5):
        steps["p%d" % k] = functools.partial(p_turn, k)
    steps["P1a"] = functools.partial(product, xh, 0, True)
    steps["P2a"] = functools.partial(product, xh, 0, False)
    steps["P1b"] = functools.partial(product, 1 - xh, 1, True)
    steps["P2b"] = product_other
    run(5)
    stores = []
    for g in range(KVH):
        lanes = pl.ds(g * HD, HD)
        for i, ref in enumerate((kout_hbm, vout_hbm)):
            stores.append(
                pltpu.make_async_copy(
                    pieces.at[2 * (g % 4) + i, g // 4], ref.at[:, lanes], out_sem.at[2 * g + i]
                )
            )
    stores.append(pltpu.make_async_copy(acc.at[0], own_hbm, out_sem.at[16]))
    for u in range(2):
        stores.append(pltpu.make_async_copy(part_r.at[u], part_hbm.at[u], out_sem.at[17 + u]))
    for store in stores[:17]:
        store.start()
    for u in range(2):
        c_copy(u).wait_recv()
        stores[17 + u].start()

    def kv_done(d, carry):
        kv_out(d).wait_send()
        forward(d).wait_send()
        dkv_out(2 * ((chip + d) % 8) + core).wait_send()
        m_copy(2 * ((chip + d) % 8) + 1 - core).wait_send()
        return carry

    lax.fori_loop(1, 8, kv_done, 0)
    to_sibling.wait_send()
    dkv_out(sibling).wait_send()
    pair_copy.wait_send()
    piece_copy.wait_send()
    for i in range(4):
        x_copy(i).wait_send()

    @pl.when(inner)
    def _():
        for i in range(4):
            on_copy(i).wait_send()

    for u in range(2):
        c_copy(u).wait_send()
        for way in range(2):
            y_copy(u, way).wait_send()
            f_copy(u, way).wait_send()
        for i in range(5):
            s_copy(u, i, core).wait_send()
    for way in range(2):
        for k in range(1, 5):
            for u in range(2):
                if hops(way, k, u):
                    z_copy(way, k, u).wait_send()
                    p_copy(way, k, u).wait_send()
    for store in stores:
        store.wait()


def local(queries, keys, values, grad_attn, segment_ids, q_weight):
    rows, width = queries.shape
    anywhere = pl.BlockSpec(memory_space=pltpu.HBM)
    dma = pltpu.SemaphoreType.DMA
    scratch = [
        pltpu.VMEM((17, 2, HALF, HD), BF16),
        pltpu.VMEM((17, HALF, PER * HALF), F32),
        pltpu.VMEM((17, HALF, PER * HALF), F32),
        pltpu.VMEM((2, PER * HALF, HD), BF16),
        pltpu.VMEM((2, PER * HALF, HD), BF16),
        pltpu.VMEM((2, PER * HALF, HD), F32),
        pltpu.VMEM((8, 8, PER * HALF), F32),
        pltpu.VMEM((16, 2, HALF, HD), BF16),
        pltpu.VMEM((16, 2, HALF, HD), BF16),
        pltpu.VMEM((16, 2, HALF, HD), BF16),
        pltpu.VMEM((2, 2, HALF, HD), F32),
        pltpu.VMEM((2 * HALF, HD), BF16),
        pltpu.VMEM((2 * HALF, HD), BF16),
        pltpu.VMEM((8, 2 * HALF, PER * HD), BF16),
        pltpu.VMEM((8, 2, 2 * HALF, HD), BF16),
        pltpu.VMEM((8, 2, 512, 512), BF16),
        pltpu.VMEM((2, 2 * HALF, 512), F32),
        pltpu.VMEM((2, HALF, 512), BF16),
        pltpu.VMEM((2, HALF, 512), BF16),
        pltpu.VMEM((32, 128), jnp.int32),
    ]
    sizes = (4, 3, 19, 8, 8, 8, 8, 16, 16, 16, 16, 2, 2, 16, 16, 16, 16, 1, 8, 8, 4, 4, 4, 4, 10, 10, 2, 2)
    own, part, key_grad, value_grad = pl.pallas_call(
        attention_kernel,
        out_shape=(
            jax.ShapeDtypeStruct((rows, width), F32),
            jax.ShapeDtypeStruct((2, rows // 2, width), BF16),
            jax.ShapeDtypeStruct((rows, KVH * HD), BF16),
            jax.ShapeDtypeStruct((rows, KVH * HD), BF16),
        ),
        in_specs=[anywhere] * 6,
        out_specs=(anywhere,) * 4,
        scratch_shapes=scratch + [dma((size,)) for size in sizes],
        compiler_params=pltpu.CompilerParams(
            collective_id=0, has_side_effects=True, vmem_limit_bytes=63 * 1024 * 1024
        ),
    )(queries, keys, values, grad_attn, segment_ids.reshape(32, 128), q_weight)
    input_grad = (own + part.reshape(rows, width).astype(F32)).astype(BF16)
    return (input_grad, key_grad, value_grad)


def solution(mesh):
    placed = (
        P("row", "col"),
        P("row", None),
        P("row", None),
        P("row", "col"),
        P(),
        P("row", "col"),
    )
    return jax.shard_map(
        local,
        mesh=mesh,
        in_specs=placed,
        out_specs=(P("row", "col"), P("row", None), P("row", None)),
        check_vma=False,
    )
```

```python
import functools
import math

import jax
import jax.numpy as jnp
from jax import lax
from jax.experimental import pallas as pl
from jax.experimental.pallas import tpu as pltpu
from jax.sharding import PartitionSpec as P

H = 64
KVH = 8
HD = 128
TOKENS = 4096
HALF = 128
PER = 4
NEG = -1e30
PLAN = (
    ("x0", "x1",),
    ("a", "x2",),
    ("x3", "i0",),
    ("i1",),
    ("i2", "i3",),
    ("m", "z1", "o", "b", "Wa", "z2", "d", "z3", "q", "z4", "px", "Wb", "La", "p1", "R1b", "P1b", "Lb", "p2", "R1a", "P1a", "R2b", "P2b", "R2a", "P2a", "p3", "p4",),
)
MESH = pl.DeviceIdType.MESH
INV_ROOT = 1.0 / math.sqrt(HD)
SCALE2 = INV_ROOT * math.log2(math.e)
F32 = jnp.float32
BF16 = jnp.bfloat16


def dot_nt(a, b):
    return lax.dot_general(a, b, (((1,), (1,)), ((), ())), preferred_element_type=F32)


def dot_nn(a, b):
    return lax.dot_general(a, b, (((1,), (0,)), ((), ())), preferred_element_type=F32)


def dot_tn(a, b):
    return lax.dot_general(a, b, (((0,), (0,)), ((), ())), preferred_element_type=F32)


def attention_kernel(
    q_hbm, k_hbm, v_hbm, g_hbm, seg_hbm, w_hbm,
    own_hbm, part_hbm, kout_hbm, vout_hbm,
    kvbuf, sbuf, dpbuf, q4, g4, dq4, stat, pbuf, mbuf, rbuf, ownf, pair_s, pair_r, dqbuf, pieces,
    wbuf, acc, part_s, part_r, seg_ref,
    load_sem, q_sem, out_sem, kv_send, kv_recv, fw_send, fw_recv, m_send, m_recv, dkv_send, dkv_recv, pair_sem,
    xp_sem, z_send, z_recv, p_send, p_recv,
    wl_sem, wx_send, wx_recv, wy_send, wy_recv, wf_send, wf_recv, ws_send, ws_recv, c_send, c_recv,
):
    s = lax.axis_index("row")
    j = lax.axis_index("col")
    chip, core = s // 2, s % 2
    xl, y = chip // 4, chip % 4
    xh, z = j // 8, j % 8
    sibling = s + 1 - 2 * core
    partner = (1 - xh) * 8 + z
    right = xh * 8 + (z + 1) % 8
    left = xh * 8 + (z + 7) % 8
    parity = z % 2
    mate = j + 1 - 2 * parity
    head = j // 2
    inner = xl != xh
    outer = xl == xh

    def remote(src, dst, ssem, rsem, row, col):
        return pltpu.make_async_remote_copy(
            src_ref=src, dst_ref=dst, send_sem=ssem, recv_sem=rsem,
            device_id=(row, col), device_id_type=MESH,
        )

    lanes = pl.ds(pl.multiple_of(head * HD, HD), HD)
    loads = []
    for u in range(2):
        slot = s if u == 0 else 16
        for i, ref in enumerate((k_hbm, v_hbm)):
            loads.append(
                pltpu.make_async_copy(
                    ref.at[pl.ds(u * HALF, HALF), lanes], kvbuf.at[slot, i], load_sem.at[2 * u + i]
                )
            )
    for copy in loads:
        copy.start()
    for u in range(2):
        for h in range(PER):
            for i, (ref, buf) in enumerate(((q_hbm, q4), (g_hbm, g4))):
                pltpu.make_async_copy(
                    ref.at[pl.ds(u * HALF, HALF), pl.ds(h * HD, HD)],
                    buf.at[u, pl.ds(h * HD, HD)],
                    q_sem.at[i],
                ).start()
    seg_load = pltpu.make_async_copy(seg_hbm, seg_ref, q_sem.at[2])
    seg_load.start()

    barrier = pltpu.get_barrier_semaphore()

    def greet(e, carry):
        pl.semaphore_signal(barrier, inc=1, device_id=((s + e) % 16, j), device_id_type=MESH)
        return carry

    lax.fori_loop(1, 16, greet, 0)
    across = (1 - xl) * 8 + y * 2 + core
    for row, col in ((s, right), (s, left), (s, partner), (across, partner)):
        pl.semaphore_signal(barrier, inc=1, device_id=(row, col), device_id_type=MESH)

    seg_load.wait()
    seg = seg_ref[...]
    counts = [jnp.sum((seg < v).astype(F32), keepdims=True) for v in (1, 2, 3)]
    lane = lax.broadcasted_iota(jnp.int32, (1, HALF), 1).astype(F32)
    bounds = []
    for u in range(2):
        block = s if u == 0 else 31 - s
        seg_q = seg_ref[pl.ds(block, 1), :]
        start = jnp.where(
            seg_q == 0, 0.0,
            jnp.where(seg_q == 1, counts[0], jnp.where(seg_q == 2, counts[1], counts[2])),
        )
        stat[4 + u, 0:1, 0:HALF] = start
        stat[4 + u, 1:2, 0:HALF] = lane + (block * HALF).astype(F32)
        stat[u] = jnp.full((8, PER * HALF), NEG, F32)

    for copy in loads:
        copy.wait()
    pltpu.make_async_copy(q4, q4, q_sem.at[0]).wait()
    pltpu.make_async_copy(g4, g4, q_sem.at[1]).wait()
    pl.semaphore_wait(barrier, 19)

    def kv_copy(d, chip_to, row_to):
        src = kvbuf.at[jnp.where(chip_to > chip, s, 16)]
        return remote(src, kvbuf.at[s], kv_send.at[d], kv_recv.at[d], row_to, j)

    def kv_out(d):
        chip_to = (chip + d) % 8
        return kv_copy(d, chip_to, chip_to * 2 + core)

    def kv_start(d, carry):
        kv_out(d).start()
        return carry

    own_half = kvbuf.at[jnp.where(core == 0, s, 16)]
    to_sibling = remote(own_half, kvbuf.at[s], kv_send.at[0], kv_recv.at[0], sibling, j)
    lax.fori_loop(1, 8, kv_start, 0)
    to_sibling.start()

    slot = 2 * y + core
    own_weight = pltpu.make_async_copy(w_hbm, wbuf.at[slot, xh], wl_sem.at[0])

    def quarter(i):
        return pl.ds(i * 128, 128)

    def x_copy(i):
        return remote(
            w_hbm.at[quarter(i)], wbuf.at[slot, xh, quarter(i)],
            wx_send.at[i], wx_recv.at[4 * xh + i], across, xl * 8 + z,
        )

    def on_copy(i):
        ref = wbuf.at[slot, 1 - xh, quarter(i)]
        return remote(ref, ref, wx_send.at[4 + i], wx_recv.at[4 * (1 - xh) + i], across, j)

    def slot_at(step, which):
        return 2 * ((y + step) % 4) + which

    def row_at(step):
        return xl * 8 + ((y + step) % 4) * 2 + core

    def x_wait(e, i):
        ref = wbuf.at[slot, e, quarter(i)]
        remote(ref, ref, wx_send.at[0], wx_recv.at[4 * e + i], across, j).wait_recv()

    def y_copy(e, way):
        ref = wbuf.at[slot, e]
        index = 2 * e + way
        return remote(ref, ref, wy_send.at[index], wy_recv.at[index], row_at(3 if way else 1), j)

    def y_wait(e, way):
        ref = wbuf.at[slot_at(1 if way else 3, core), e]
        index = 2 * e + way
        remote(ref, ref, wy_send.at[index], wy_recv.at[index], s, right).wait_recv()

    def f_ref(step, e, way):
        return wbuf.at[slot_at(step, core), e, pl.ds(way * 256, 256)]

    def f_copy(e, way):
        ref = f_ref(1 if way else 3, e, way)
        index = 2 * e + way
        return remote(ref, ref, wf_send.at[index], wf_recv.at[index], row_at(3 if way else 1), j)

    def f_wait(e, way):
        ref = f_ref(2, e, way)
        index = 2 * e + way
        remote(ref, ref, wf_send.at[index], wf_recv.at[index], s, right).wait_recv()

    def s_copy(e, i, which):
        if i < 3:
            ref = wbuf.at[slot_at((0, 3, 1)[i], which), e]
        else:
            ref = wbuf.at[slot_at(2, which), e, pl.ds((i - 3) * 256, 256)]
        index = 5 * e + i
        return remote(ref, ref, ws_send.at[index], ws_recv.at[index], sibling, j)

    def y_start(e, i, ref):
        for way in range(2):
            index = 2 * e + way
            remote(
                ref, wbuf.at[slot, e, quarter(i)], wy_send.at[index], wy_recv.at[index],
                row_at(3 if way else 1), j,
            ).start()

    steps = {}

    def run(stage):
        for name in PLAN[stage]:
            steps[name]()

    def send_own():
        @pl.when(outer)
        def _():
            own_weight.start()
            for i in range(4):
                y_start(xh, i, w_hbm.at[quarter(i)])

    def weight_inner(i):
        @pl.when(inner)
        def _():
            x_wait(1 - xh, i)
            on_copy(i).start()
            x_wait(xh, i)
            y_start(xh, i, wbuf.at[slot, xh, quarter(i)])
            if i == 3:
                s_copy(xh, 0, core).start()

    def weight_outer():
        @pl.when(outer)
        def _():
            own_weight.wait()
            s_copy(xh, 0, core).start()
            for i in range(4):
                x_wait(1 - xh, i)

    def send_other():
        y_copy(1 - xh, 0).start()
        y_copy(1 - xh, 1).start()
        s_copy(1 - xh, 0, core).start()

    for i in range(4):
        steps["x%d" % i] = x_copy(i).start
        steps["i%d" % i] = functools.partial(weight_inner, i)
    steps["a"] = send_own
    steps["o"] = weight_outer
    steps["b"] = send_other

    def weight_pass(e):
        for way in range(2):
            y_wait(e, way)
            f_copy(e, way).start()
            s_copy(e, 1 + way, core).start()

    def weight_last(e):
        for way in range(2):
            f_wait(e, way)
            s_copy(e, 3 + way, core).start()

    def weight_ready(e, first, last):
        for i in range(first, last):
            s_copy(e, i, 1 - core).wait_recv()

    for name, e in (("a", xh), ("b", 1 - xh)):
        steps["W" + name] = functools.partial(weight_pass, e)
        steps["L" + name] = functools.partial(weight_last, e)
        steps["R1" + name] = functools.partial(weight_ready, e, 0, 3)
        steps["R2" + name] = functools.partial(weight_ready, e, 3, 5)
    run(0)

    sub = lax.broadcasted_iota(jnp.int32, (HALF, HALF), 0).astype(F32)

    def pass_one(t):
        u = jnp.where(t > s, 1, 0)
        block = jnp.where(t > s, jnp.where(t == 16, 31 - s, 31 - t), t)
        key_place = sub + (block * HALF).astype(F32)
        start = stat[4 + u, 0:1, 0:HALF]
        place = stat[4 + u, 1:2, 0:HALF]
        bias = jnp.where((key_place >= start) & (key_place <= place), 0.0, NEG)
        scores = dot_nt(kvbuf[t, 0], q4[u])
        for h in range(PER):
            part = scores[:, h * HALF:(h + 1) * HALF] * SCALE2 + bias
            sbuf[t, :, h * HALF:(h + 1) * HALF] = part
            top = jnp.max(part.reshape(16, 8, HALF), axis=0)
            stat[u, :, h * HALF:(h + 1) * HALF] = jnp.maximum(
                stat[u, :, h * HALF:(h + 1) * HALF], top
            )
        dpbuf[t] = dot_nt(kvbuf[t, 1], g4[u])

    pass_one(s)
    pass_one(16)

    def forward(d):
        origin = ((chip + 8 - d) % 8) * 2 + core
        return remote(kvbuf.at[origin], kvbuf.at[origin], fw_send.at[d], fw_recv.at[d], sibling, j)

    def arrive(d, carry):
        origin = ((chip + 8 - d) % 8) * 2 + core
        remote(
            kvbuf.at[origin], kvbuf.at[origin], kv_send.at[d], kv_recv.at[d], sibling, j
        ).wait_recv()
        forward(d).start()
        pass_one(origin)
        return carry

    lax.fori_loop(1, 8, arrive, 0)

    run(1)
    remote(
        kvbuf.at[sibling], kvbuf.at[sibling], kv_send.at[0], kv_recv.at[0], sibling, j
    ).wait_recv()
    pass_one(sibling)

    def arrive_two(d, carry):
        origin = ((chip + 8 - d) % 8) * 2 + 1 - core
        remote(
            kvbuf.at[origin], kvbuf.at[origin], fw_send.at[d], fw_recv.at[d], sibling, j
        ).wait_recv()
        pass_one(origin)
        return carry

    lax.fori_loop(1, 8, arrive_two, 0)

    run(2)

    for u in range(2):
        top = jnp.max(stat[u], axis=0, keepdims=True)
        stat[u] = jnp.broadcast_to(top, (8, PER * HALF))
        stat[2 + u] = jnp.zeros((8, PER * HALF), F32)
        stat[6 + u] = jnp.zeros((8, PER * HALF), F32)

    def pass_two(t, carry):
        u = jnp.where(t > s, 1, 0)
        for h in range(PER):
            cols = slice(h * HALF, (h + 1) * HALF)
            top = stat[u, 0:1, cols]
            expo = jnp.exp2(sbuf[t, :, cols] - top)
            sbuf[t, :, cols] = expo
            stat[2 + u, :, cols] += jnp.sum(expo.reshape(16, 8, HALF), axis=0)
            stat[6 + u, :, cols] += jnp.sum((expo * dpbuf[t, :, cols]).reshape(16, 8, HALF), axis=0)
        return carry

    lax.fori_loop(0, 17, pass_two, 0)

    run(3)
    for u in range(2):
        total = jnp.sum(stat[2 + u], axis=0, keepdims=True)
        inverse = 1.0 / total
        delta = jnp.sum(stat[6 + u], axis=0, keepdims=True) * inverse
        stat[2 + u, 0:1, :] = inverse
        stat[6 + u, 0:1, :] = delta
        dq4[u] = jnp.zeros((PER * HALF, HD), F32)

    def m_copy(t):
        return remote(pbuf.at[t], mbuf.at[t], m_send.at[t], m_recv.at[t], sibling, j)

    def dkv_out(t):
        return remote(pbuf.at[t], rbuf.at[s], dkv_send.at[t], dkv_recv.at[s], t, j)

    def pass_three(t, carry):
        u = jnp.where(t > s, 1, 0)
        inverse = stat[2 + u, 0:1, :]
        delta = stat[6 + u, 0:1, :]
        probs = sbuf[t] * inverse
        dscore = (probs * (dpbuf[t] - delta)).astype(BF16)
        key_part = dot_nn(dscore, q4[u])
        value_part = dot_nn(probs.astype(BF16), g4[u])
        dq4[u] += dot_tn(dscore, kvbuf[t, 0])
        mine = (t == s) | (t == 16)

        @pl.when(mine)
        def _():
            ownf[u, 0] = key_part
            ownf[u, 1] = value_part

        @pl.when(jnp.logical_not(mine))
        def _():
            pbuf[t, 0] = key_part.astype(BF16)
            pbuf[t, 1] = value_part.astype(BF16)

            @pl.when(t == sibling)
            def _():
                dkv_out(t).start()

            @pl.when((t != sibling) & (t % 2 != core))
            def _():
                m_copy(t).start()

        return carry

    def z_copy(way, k, u):
        origin = (z + 8 - (k - 1)) % 8 if way == 0 else (z + (k - 1)) % 8
        src = dqbuf.at[origin, pl.ds(u * HALF, HALF)]
        index = (way * 4 + (k - 1)) * 2 + u
        return remote(src, src, z_send.at[index], z_recv.at[index], s, right if way == 0 else left)

    def z_wait(way, k, u):
        origin = (z + 8 - k) % 8 if way == 0 else (z + k) % 8
        dst = dqbuf.at[origin, pl.ds(u * HALF, HALF)]
        index = (way * 4 + (k - 1)) * 2 + u
        remote(dst, dst, z_send.at[index], z_recv.at[index], s, right).wait_recv()

    def hops(way, k, u):
        return k <= 3 or u == way

    def z_turn(k):
        for u in (1, 0):
            for way in range(2):
                if hops(way, k, u):
                    z_wait(way, k, u)
                    if k < 4 and hops(way, k + 1, u):
                        z_copy(way, k + 1, u).start()

    for u, first, last in ((1, s + 1, 17), (0, 0, s + 1)):
        lax.fori_loop(first, last, pass_three, 0)
        for h in range(PER):
            dqbuf[z, u * HALF:(u + 1) * HALF, h * HD:(h + 1) * HD] = (
                dq4[u, h * HD:(h + 1) * HD, :] * INV_ROOT
            ).astype(BF16)
        z_copy(0, 1, u).start()
        z_copy(1, 1, u).start()
        if u == 1:
            run(4)

    def merge(d, carry):
        t = 2 * ((chip + d) % 8) + core
        remote(pbuf.at[t], mbuf.at[t], m_send.at[t], m_recv.at[t], sibling, j).wait_recv()
        for i in range(2):
            pbuf[t, i] = (pbuf[t, i].astype(F32) + mbuf[t, i].astype(F32)).astype(BF16)
        dkv_out(t).start()
        return carry

    steps["m"] = lambda: lax.fori_loop(1, 8, merge, 0)
    for k in range(1, 5):
        steps["z%d" % k] = functools.partial(z_turn, k)

    def dkv_take(r):
        remote(rbuf.at[r], rbuf.at[r], dkv_send.at[r], dkv_recv.at[r], s, right).wait_recv()
        u = jnp.where(r > s, 0, 1)
        for i in range(2):
            ownf[u, i] += rbuf[r, i].astype(F32)

    def take(d, carry):
        dkv_take(2 * ((chip + 8 - d) % 8) + core)
        return carry

    pair_copy = remote(pair_s, pair_r, pair_sem.at[0], pair_sem.at[1], s, mate)
    piece = pieces.at[z, xh]
    piece_copy = remote(piece, piece, xp_sem.at[0], xp_sem.at[1], s, partner)

    def gather_rows():
        dkv_take(sibling)
        lax.fori_loop(1, 8, take, 0)
        for u in range(2):
            pair_s[u * HALF:(u + 1) * HALF, :] = ownf[u, 1 - parity].astype(BF16)
        pair_copy.start()

    def make_piece():
        pair_copy.wait_recv()
        factor = jnp.where(parity == 0, INV_ROOT, 1.0).astype(F32)
        for u in range(2):
            rows = slice(u * HALF, (u + 1) * HALF)
            pieces[z, xh, rows, :] = (
                (ownf[u, parity] + pair_r[rows, :].astype(F32)) * factor
            ).astype(BF16)
        piece_copy.start()

    def p_copy(way, k, i):
        origin = (z + 8 - (k - 1)) % 8 if way == 0 else (z + (k - 1)) % 8
        src = pieces.at[origin, i]
        index = (way * 4 + (k - 1)) * 2 + i
        return remote(src, src, p_send.at[index], p_recv.at[index], s, right if way == 0 else left)

    def p_wait(way, k, i):
        origin = (z + 8 - k) % 8 if way == 0 else (z + k) % 8
        dst = pieces.at[origin, i]
        index = (way * 4 + (k - 1)) * 2 + i
        remote(dst, dst, p_send.at[index], p_recv.at[index], s, right).wait_recv()

    def p_begin():
        other = pieces.at[z, 1 - xh]
        remote(other, other, xp_sem.at[0], xp_sem.at[1], s, partner).wait_recv()
        for i in range(2):
            p_copy(0, 1, i).start()
            p_copy(1, 1, i).start()

    def p_turn(k):
        for i in (1, 0):
            for way in range(2):
                if hops(way, k, i):
                    p_wait(way, k, i)
                    if k < 4 and hops(way, k + 1, i):
                        p_copy(way, k + 1, i).start()

    def product(e, i, near):
        if near:
            acc[i] = jnp.zeros((2 * HALF, 512), F32)

        def add(n, carry):
            step = n // 2 + n // 4 if near else 2
            zz = 2 * ((y + step) % 4) + n % 2
            acc[i] += dot_nn(dqbuf[zz], wbuf[zz, e])
            return carry

        lax.fori_loop(0, 6 if near else 2, add, 0)

    def c_copy(u):
        return remote(part_s.at[u], part_r.at[u], c_send.at[u], c_recv.at[u], s, partner)

    def product_other():
        product(1 - xh, 1, False)
        for u in range(2):
            part_s[u] = acc[1, u * HALF:(u + 1) * HALF, :].astype(BF16)
            c_copy(u).start()

    steps["d"] = gather_rows
    steps["q"] = make_piece
    steps["px"] = p_begin
    for k in range(1, 5):
        steps["p%d" % k] = functools.partial(p_turn, k)
    steps["P1a"] = functools.partial(product, xh, 0, True)
    steps["P2a"] = functools.partial(product, xh, 0, False)
    steps["P1b"] = functools.partial(product, 1 - xh, 1, True)
    steps["P2b"] = product_other
    run(5)
    stores = []
    for g in range(KVH):
        lanes = pl.ds(g * HD, HD)
        for i, ref in enumerate((kout_hbm, vout_hbm)):
            stores.append(
                pltpu.make_async_copy(
                    pieces.at[2 * (g % 4) + i, g // 4], ref.at[:, lanes], out_sem.at[2 * g + i]
                )
            )
    stores.append(pltpu.make_async_copy(acc.at[0], own_hbm, out_sem.at[16]))
    for u in range(2):
        stores.append(pltpu.make_async_copy(part_r.at[u], part_hbm.at[u], out_sem.at[17 + u]))
    for store in stores[:17]:
        store.start()
    for u in range(2):
        c_copy(u).wait_recv()
        stores[17 + u].start()

    def kv_done(d, carry):
        kv_out(d).wait_send()
        forward(d).wait_send()
        dkv_out(2 * ((chip + d) % 8) + core).wait_send()
        m_copy(2 * ((chip + d) % 8) + 1 - core).wait_send()
        return carry

    lax.fori_loop(1, 8, kv_done, 0)
    to_sibling.wait_send()
    dkv_out(sibling).wait_send()
    pair_copy.wait_send()
    piece_copy.wait_send()
    for i in range(4):
        x_copy(i).wait_send()

    @pl.when(inner)
    def _():
        for i in range(4):
            on_copy(i).wait_send()

    for u in range(2):
        c_copy(u).wait_send()
        for way in range(2):
            y_copy(u, way).wait_send()
            f_copy(u, way).wait_send()
        for i in range(5):
            s_copy(u, i, core).wait_send()
    for way in range(2):
        for k in range(1, 5):
            for u in range(2):
                if hops(way, k, u):
                    z_copy(way, k, u).wait_send()
                    p_copy(way, k, u).wait_send()
    for store in stores:
        store.wait()


def local(queries, keys, values, grad_attn, segment_ids, q_weight):
    rows, width = queries.shape
    anywhere = pl.BlockSpec(memory_space=pltpu.HBM)
    dma = pltpu.SemaphoreType.DMA
    scratch = [
        pltpu.VMEM((17, 2, HALF, HD), BF16),
        pltpu.VMEM((17, HALF, PER * HALF), F32),
        pltpu.VMEM((17, HALF, PER * HALF), F32),
        pltpu.VMEM((2, PER * HALF, HD), BF16),
        pltpu.VMEM((2, PER * HALF, HD), BF16),
        pltpu.VMEM((2, PER * HALF, HD), F32),
        pltpu.VMEM((8, 8, PER * HALF), F32),
        pltpu.VMEM((16, 2, HALF, HD), BF16),
        pltpu.VMEM((16, 2, HALF, HD), BF16),
        pltpu.VMEM((16, 2, HALF, HD), BF16),
        pltpu.VMEM((2, 2, HALF, HD), F32),
        pltpu.VMEM((2 * HALF, HD), BF16),
        pltpu.VMEM((2 * HALF, HD), BF16),
        pltpu.VMEM((8, 2 * HALF, PER * HD), BF16),
        pltpu.VMEM((8, 2, 2 * HALF, HD), BF16),
        pltpu.VMEM((8, 2, 512, 512), BF16),
        pltpu.VMEM((2, 2 * HALF, 512), F32),
        pltpu.VMEM((2, HALF, 512), BF16),
        pltpu.VMEM((2, HALF, 512), BF16),
        pltpu.VMEM((32, 128), jnp.int32),
    ]
    sizes = (4, 3, 19, 8, 8, 8, 8, 16, 16, 16, 16, 2, 2, 16, 16, 16, 16, 1, 8, 8, 4, 4, 4, 4, 10, 10, 2, 2)
    own, part, key_grad, value_grad = pl.pallas_call(
        attention_kernel,
        out_shape=(
            jax.ShapeDtypeStruct((rows, width), F32),
            jax.ShapeDtypeStruct((2, rows // 2, width), BF16),
            jax.ShapeDtypeStruct((rows, KVH * HD), BF16),
            jax.ShapeDtypeStruct((rows, KVH * HD), BF16),
        ),
        in_specs=[anywhere] * 6,
        out_specs=(anywhere,) * 4,
        scratch_shapes=scratch + [dma((size,)) for size in sizes],
        compiler_params=pltpu.CompilerParams(
            collective_id=0, has_side_effects=True, vmem_limit_bytes=63 * 1024 * 1024
        ),
    )(queries, keys, values, grad_attn, segment_ids.reshape(32, 128), q_weight)
    input_grad = (own + part.reshape(rows, width).astype(F32)).astype(BF16)
    return (input_grad, key_grad, value_grad)


def solution(mesh):
    placed = (
        P("row", "col"),
        P("row", None),
        P("row", None),
        P("row", "col"),
        P(),
        P("row", "col"),
    )
    return jax.shard_map(
        local,
        mesh=mesh,
        in_specs=placed,
        out_specs=(P("row", "col"), P("row", None), P("row", None)),
        check_vma=False,
    )
```

```python
import functools
import math

import jax
import jax.numpy as jnp
from jax import lax
from jax.experimental import pallas as pl
from jax.experimental.pallas import tpu as pltpu
from jax.sharding import PartitionSpec as P

H = 64
KVH = 8
HD = 128
TOKENS = 4096
HALF = 128
PER = 4
NEG = -1e30
PLAN = (
    ("x0", "x1",),
    ("a", "x2",),
    ("x3", "i0",),
    ("i1",),
    ("i2", "i3",),
    ("m", "z1", "o", "b", "Wa", "z2", "d", "z3", "q", "z4", "px", "Wb", "La", "p1", "R1b", "P1b", "Lb", "p2", "R2b", "P2b", "p3", "R1a", "P1a", "R2a", "P2a", "p4",),
)
MESH = pl.DeviceIdType.MESH
INV_ROOT = 1.0 / math.sqrt(HD)
SCALE2 = INV_ROOT * math.log2(math.e)
F32 = jnp.float32
BF16 = jnp.bfloat16


def dot_nt(a, b):
    return lax.dot_general(a, b, (((1,), (1,)), ((), ())), preferred_element_type=F32)


def dot_nn(a, b):
    return lax.dot_general(a, b, (((1,), (0,)), ((), ())), preferred_element_type=F32)


def dot_tn(a, b):
    return lax.dot_general(a, b, (((0,), (0,)), ((), ())), preferred_element_type=F32)


def attention_kernel(
    q_hbm, k_hbm, v_hbm, g_hbm, seg_hbm, w_hbm,
    own_hbm, part_hbm, kout_hbm, vout_hbm,
    kvbuf, sbuf, dpbuf, q4, g4, dq4, stat, pbuf, mbuf, rbuf, ownf, pair_s, pair_r, dqbuf, pieces,
    wbuf, acc, part_s, part_r, seg_ref,
    load_sem, q_sem, out_sem, kv_send, kv_recv, fw_send, fw_recv, m_send, m_recv, dkv_send, dkv_recv, pair_sem,
    xp_sem, z_send, z_recv, p_send, p_recv,
    wl_sem, wx_send, wx_recv, wy_send, wy_recv, wf_send, wf_recv, ws_send, ws_recv, c_send, c_recv,
):
    s = lax.axis_index("row")
    j = lax.axis_index("col")
    chip, core = s // 2, s % 2
    xl, y = chip // 4, chip % 4
    xh, z = j // 8, j % 8
    sibling = s + 1 - 2 * core
    partner = (1 - xh) * 8 + z
    right = xh * 8 + (z + 1) % 8
    left = xh * 8 + (z + 7) % 8
    parity = z % 2
    mate = j + 1 - 2 * parity
    head = j // 2
    inner = xl != xh
    outer = xl == xh

    def remote(src, dst, ssem, rsem, row, col):
        return pltpu.make_async_remote_copy(
            src_ref=src, dst_ref=dst, send_sem=ssem, recv_sem=rsem,
            device_id=(row, col), device_id_type=MESH,
        )

    lanes = pl.ds(pl.multiple_of(head * HD, HD), HD)
    loads = []
    for u in range(2):
        slot = s if u == 0 else 16
        for i, ref in enumerate((k_hbm, v_hbm)):
            loads.append(
                pltpu.make_async_copy(
                    ref.at[pl.ds(u * HALF, HALF), lanes], kvbuf.at[slot, i], load_sem.at[2 * u + i]
                )
            )
    for copy in loads:
        copy.start()
    for u in range(2):
        for h in range(PER):
            for i, (ref, buf) in enumerate(((q_hbm, q4), (g_hbm, g4))):
                pltpu.make_async_copy(
                    ref.at[pl.ds(u * HALF, HALF), pl.ds(h * HD, HD)],
                    buf.at[u, pl.ds(h * HD, HD)],
                    q_sem.at[i],
                ).start()
    seg_load = pltpu.make_async_copy(seg_hbm, seg_ref, q_sem.at[2])
    seg_load.start()

    barrier = pltpu.get_barrier_semaphore()

    def greet(e, carry):
        pl.semaphore_signal(barrier, inc=1, device_id=((s + e) % 16, j), device_id_type=MESH)
        return carry

    lax.fori_loop(1, 16, greet, 0)
    across = (1 - xl) * 8 + y * 2 + core
    for row, col in ((s, right), (s, left), (s, partner), (across, partner)):
        pl.semaphore_signal(barrier, inc=1, device_id=(row, col), device_id_type=MESH)

    seg_load.wait()
    seg = seg_ref[...]
    counts = [jnp.sum((seg < v).astype(F32), keepdims=True) for v in (1, 2, 3)]
    lane = lax.broadcasted_iota(jnp.int32, (1, HALF), 1).astype(F32)
    bounds = []
    for u in range(2):
        block = s if u == 0 else 31 - s
        seg_q = seg_ref[pl.ds(block, 1), :]
        start = jnp.where(
            seg_q == 0, 0.0,
            jnp.where(seg_q == 1, counts[0], jnp.where(seg_q == 2, counts[1], counts[2])),
        )
        stat[4 + u, 0:1, 0:HALF] = start
        stat[4 + u, 1:2, 0:HALF] = lane + (block * HALF).astype(F32)
        stat[u] = jnp.full((8, PER * HALF), NEG, F32)

    for copy in loads:
        copy.wait()
    pltpu.make_async_copy(q4, q4, q_sem.at[0]).wait()
    pltpu.make_async_copy(g4, g4, q_sem.at[1]).wait()
    pl.semaphore_wait(barrier, 19)

    def kv_copy(d, chip_to, row_to):
        src = kvbuf.at[jnp.where(chip_to > chip, s, 16)]
        return remote(src, kvbuf.at[s], kv_send.at[d], kv_recv.at[d], row_to, j)

    def kv_out(d):
        chip_to = (chip + d) % 8
        return kv_copy(d, chip_to, chip_to * 2 + core)

    def kv_start(d, carry):
        kv_out(d).start()
        return carry

    own_half = kvbuf.at[jnp.where(core == 0, s, 16)]
    to_sibling = remote(own_half, kvbuf.at[s], kv_send.at[0], kv_recv.at[0], sibling, j)
    lax.fori_loop(1, 8, kv_start, 0)
    to_sibling.start()

    slot = 2 * y + core
    own_weight = pltpu.make_async_copy(w_hbm, wbuf.at[slot, xh], wl_sem.at[0])

    def quarter(i):
        return pl.ds(i * 128, 128)

    def x_copy(i):
        return remote(
            w_hbm.at[quarter(i)], wbuf.at[slot, xh, quarter(i)],
            wx_send.at[i], wx_recv.at[4 * xh + i], across, xl * 8 + z,
        )

    def on_copy(i):
        ref = wbuf.at[slot, 1 - xh, quarter(i)]
        return remote(ref, ref, wx_send.at[4 + i], wx_recv.at[4 * (1 - xh) + i], across, j)

    def slot_at(step, which):
        return 2 * ((y + step) % 4) + which

    def row_at(step):
        return xl * 8 + ((y + step) % 4) * 2 + core

    def x_wait(e, i):
        ref = wbuf.at[slot, e, quarter(i)]
        remote(ref, ref, wx_send.at[0], wx_recv.at[4 * e + i], across, j).wait_recv()

    def y_copy(e, way):
        ref = wbuf.at[slot, e]
        index = 2 * e + way
        return remote(ref, ref, wy_send.at[index], wy_recv.at[index], row_at(3 if way else 1), j)

    def y_wait(e, way):
        ref = wbuf.at[slot_at(1 if way else 3, core), e]
        index = 2 * e + way
        remote(ref, ref, wy_send.at[index], wy_recv.at[index], s, right).wait_recv()

    def f_ref(step, e, way):
        return wbuf.at[slot_at(step, core), e, pl.ds(way * 256, 256)]

    def f_copy(e, way):
        ref = f_ref(1 if way else 3, e, way)
        index = 2 * e + way
        return remote(ref, ref, wf_send.at[index], wf_recv.at[index], row_at(3 if way else 1), j)

    def f_wait(e, way):
        ref = f_ref(2, e, way)
        index = 2 * e + way
        remote(ref, ref, wf_send.at[index], wf_recv.at[index], s, right).wait_recv()

    def s_copy(e, i, which):
        if i < 3:
            ref = wbuf.at[slot_at((0, 3, 1)[i], which), e]
        else:
            ref = wbuf.at[slot_at(2, which), e, pl.ds((i - 3) * 256, 256)]
        index = 5 * e + i
        return remote(ref, ref, ws_send.at[index], ws_recv.at[index], sibling, j)

    def y_start(e, i, ref):
        for way in range(2):
            index = 2 * e + way
            remote(
                ref, wbuf.at[slot, e, quarter(i)], wy_send.at[index], wy_recv.at[index],
                row_at(3 if way else 1), j,
            ).start()

    steps = {}

    def run(stage):
        for name in PLAN[stage]:
            steps[name]()

    def send_own():
        @pl.when(outer)
        def _():
            own_weight.start()
            for i in range(4):
                y_start(xh, i, w_hbm.at[quarter(i)])

    def weight_inner(i):
        @pl.when(inner)
        def _():
            x_wait(1 - xh, i)
            on_copy(i).start()
            x_wait(xh, i)
            y_start(xh, i, wbuf.at[slot, xh, quarter(i)])
            if i == 3:
                s_copy(xh, 0, core).start()

    def weight_outer():
        @pl.when(outer)
        def _():
            own_weight.wait()
            s_copy(xh, 0, core).start()
            for i in range(4):
                x_wait(1 - xh, i)

    def send_other():
        y_copy(1 - xh, 0).start()
        y_copy(1 - xh, 1).start()
        s_copy(1 - xh, 0, core).start()

    for i in range(4):
        steps["x%d" % i] = x_copy(i).start
        steps["i%d" % i] = functools.partial(weight_inner, i)
    steps["a"] = send_own
    steps["o"] = weight_outer
    steps["b"] = send_other

    def weight_pass(e):
        for way in range(2):
            y_wait(e, way)
            f_copy(e, way).start()
            s_copy(e, 1 + way, core).start()

    def weight_last(e):
        for way in range(2):
            f_wait(e, way)
            s_copy(e, 3 + way, core).start()

    def weight_ready(e, first, last):
        for i in range(first, last):
            s_copy(e, i, 1 - core).wait_recv()

    for name, e in (("a", xh), ("b", 1 - xh)):
        steps["W" + name] = functools.partial(weight_pass, e)
        steps["L" + name] = functools.partial(weight_last, e)
        steps["R1" + name] = functools.partial(weight_ready, e, 0, 3)
        steps["R2" + name] = functools.partial(weight_ready, e, 3, 5)
    run(0)

    sub = lax.broadcasted_iota(jnp.int32, (HALF, HALF), 0).astype(F32)

    def pass_one(t):
        u = jnp.where(t > s, 1, 0)
        block = jnp.where(t > s, jnp.where(t == 16, 31 - s, 31 - t), t)
        key_place = sub + (block * HALF).astype(F32)
        start = stat[4 + u, 0:1, 0:HALF]
        place = stat[4 + u, 1:2, 0:HALF]
        bias = jnp.where((key_place >= start) & (key_place <= place), 0.0, NEG)
        scores = dot_nt(kvbuf[t, 0], q4[u])
        for h in range(PER):
            part = scores[:, h * HALF:(h + 1) * HALF] * SCALE2 + bias
            sbuf[t, :, h * HALF:(h + 1) * HALF] = part
            top = jnp.max(part.reshape(16, 8, HALF), axis=0)
            stat[u, :, h * HALF:(h + 1) * HALF] = jnp.maximum(
                stat[u, :, h * HALF:(h + 1) * HALF], top
            )
        dpbuf[t] = dot_nt(kvbuf[t, 1], g4[u])

    pass_one(s)
    pass_one(16)

    def forward(d):
        origin = ((chip + 8 - d) % 8) * 2 + core
        return remote(kvbuf.at[origin], kvbuf.at[origin], fw_send.at[d], fw_recv.at[d], sibling, j)

    def arrive(d, carry):
        origin = ((chip + 8 - d) % 8) * 2 + core
        remote(
            kvbuf.at[origin], kvbuf.at[origin], kv_send.at[d], kv_recv.at[d], sibling, j
        ).wait_recv()
        forward(d).start()
        pass_one(origin)
        return carry

    lax.fori_loop(1, 8, arrive, 0)

    run(1)
    remote(
        kvbuf.at[sibling], kvbuf.at[sibling], kv_send.at[0], kv_recv.at[0], sibling, j
    ).wait_recv()
    pass_one(sibling)

    def arrive_two(d, carry):
        origin = ((chip + 8 - d) % 8) * 2 + 1 - core
        remote(
            kvbuf.at[origin], kvbuf.at[origin], fw_send.at[d], fw_recv.at[d], sibling, j
        ).wait_recv()
        pass_one(origin)
        return carry

    lax.fori_loop(1, 8, arrive_two, 0)

    run(2)

    for u in range(2):
        top = jnp.max(stat[u], axis=0, keepdims=True)
        stat[u] = jnp.broadcast_to(top, (8, PER * HALF))
        stat[2 + u] = jnp.zeros((8, PER * HALF), F32)
        stat[6 + u] = jnp.zeros((8, PER * HALF), F32)

    def pass_two(t, carry):
        u = jnp.where(t > s, 1, 0)
        for h in range(PER):
            cols = slice(h * HALF, (h + 1) * HALF)
            top = stat[u, 0:1, cols]
            expo = jnp.exp2(sbuf[t, :, cols] - top)
            sbuf[t, :, cols] = expo
            stat[2 + u, :, cols] += jnp.sum(expo.reshape(16, 8, HALF), axis=0)
            stat[6 + u, :, cols] += jnp.sum((expo * dpbuf[t, :, cols]).reshape(16, 8, HALF), axis=0)
        return carry

    lax.fori_loop(0, 17, pass_two, 0)

    run(3)
    for u in range(2):
        total = jnp.sum(stat[2 + u], axis=0, keepdims=True)
        inverse = 1.0 / total
        delta = jnp.sum(stat[6 + u], axis=0, keepdims=True) * inverse
        stat[2 + u, 0:1, :] = inverse
        stat[6 + u, 0:1, :] = delta
        dq4[u] = jnp.zeros((PER * HALF, HD), F32)

    def m_copy(t):
        return remote(pbuf.at[t], mbuf.at[t], m_send.at[t], m_recv.at[t], sibling, j)

    def dkv_out(t):
        return remote(pbuf.at[t], rbuf.at[s], dkv_send.at[t], dkv_recv.at[s], t, j)

    def pass_three(t, carry):
        u = jnp.where(t > s, 1, 0)
        inverse = stat[2 + u, 0:1, :]
        delta = stat[6 + u, 0:1, :]
        probs = sbuf[t] * inverse
        dscore = (probs * (dpbuf[t] - delta)).astype(BF16)
        key_part = dot_nn(dscore, q4[u])
        value_part = dot_nn(probs.astype(BF16), g4[u])
        dq4[u] += dot_tn(dscore, kvbuf[t, 0])
        mine = (t == s) | (t == 16)

        @pl.when(mine)
        def _():
            ownf[u, 0] = key_part
            ownf[u, 1] = value_part

        @pl.when(jnp.logical_not(mine))
        def _():
            pbuf[t, 0] = key_part.astype(BF16)
            pbuf[t, 1] = value_part.astype(BF16)

            @pl.when(t == sibling)
            def _():
                dkv_out(t).start()

            @pl.when((t != sibling) & (t % 2 != core))
            def _():
                m_copy(t).start()

        return carry

    def z_copy(way, k, u):
        origin = (z + 8 - (k - 1)) % 8 if way == 0 else (z + (k - 1)) % 8
        src = dqbuf.at[origin, pl.ds(u * HALF, HALF)]
        index = (way * 4 + (k - 1)) * 2 + u
        return remote(src, src, z_send.at[index], z_recv.at[index], s, right if way == 0 else left)

    def z_wait(way, k, u):
        origin = (z + 8 - k) % 8 if way == 0 else (z + k) % 8
        dst = dqbuf.at[origin, pl.ds(u * HALF, HALF)]
        index = (way * 4 + (k - 1)) * 2 + u
        remote(dst, dst, z_send.at[index], z_recv.at[index], s, right).wait_recv()

    def hops(way, k, u):
        return k <= 3 or u == way

    def z_turn(k):
        for u in (1, 0):
            for way in range(2):
                if hops(way, k, u):
                    z_wait(way, k, u)
                    if k < 4 and hops(way, k + 1, u):
                        z_copy(way, k + 1, u).start()

    for u, first, last in ((1, s + 1, 17), (0, 0, s + 1)):
        lax.fori_loop(first, last, pass_three, 0)
        for h in range(PER):
            dqbuf[z, u * HALF:(u + 1) * HALF, h * HD:(h + 1) * HD] = (
                dq4[u, h * HD:(h + 1) * HD, :] * INV_ROOT
            ).astype(BF16)
        z_copy(0, 1, u).start()
        z_copy(1, 1, u).start()
        if u == 1:
            run(4)

    def merge(d, carry):
        t = 2 * ((chip + d) % 8) + core
        remote(pbuf.at[t], mbuf.at[t], m_send.at[t], m_recv.at[t], sibling, j).wait_recv()
        for i in range(2):
            pbuf[t, i] = (pbuf[t, i].astype(F32) + mbuf[t, i].astype(F32)).astype(BF16)
        dkv_out(t).start()
        return carry

    steps["m"] = lambda: lax.fori_loop(1, 8, merge, 0)
    for k in range(1, 5):
        steps["z%d" % k] = functools.partial(z_turn, k)

    def dkv_take(r):
        remote(rbuf.at[r], rbuf.at[r], dkv_send.at[r], dkv_recv.at[r], s, right).wait_recv()
        u = jnp.where(r > s, 0, 1)
        for i in range(2):
            ownf[u, i] += rbuf[r, i].astype(F32)

    def take(d, carry):
        dkv_take(2 * ((chip + 8 - d) % 8) + core)
        return carry

    pair_copy = remote(pair_s, pair_r, pair_sem.at[0], pair_sem.at[1], s, mate)
    piece = pieces.at[z, xh]
    piece_copy = remote(piece, piece, xp_sem.at[0], xp_sem.at[1], s, partner)

    def gather_rows():
        dkv_take(sibling)
        lax.fori_loop(1, 8, take, 0)
        for u in range(2):
            pair_s[u * HALF:(u + 1) * HALF, :] = ownf[u, 1 - parity].astype(BF16)
        pair_copy.start()

    def make_piece():
        pair_copy.wait_recv()
        factor = jnp.where(parity == 0, INV_ROOT, 1.0).astype(F32)
        for u in range(2):
            rows = slice(u * HALF, (u + 1) * HALF)
            pieces[z, xh, rows, :] = (
                (ownf[u, parity] + pair_r[rows, :].astype(F32)) * factor
            ).astype(BF16)
        piece_copy.start()

    def p_copy(way, k, i):
        origin = (z + 8 - (k - 1)) % 8 if way == 0 else (z + (k - 1)) % 8
        src = pieces.at[origin, i]
        index = (way * 4 + (k - 1)) * 2 + i
        return remote(src, src, p_send.at[index], p_recv.at[index], s, right if way == 0 else left)

    def p_wait(way, k, i):
        origin = (z + 8 - k) % 8 if way == 0 else (z + k) % 8
        dst = pieces.at[origin, i]
        index = (way * 4 + (k - 1)) * 2 + i
        remote(dst, dst, p_send.at[index], p_recv.at[index], s, right).wait_recv()

    def p_begin():
        other = pieces.at[z, 1 - xh]
        remote(other, other, xp_sem.at[0], xp_sem.at[1], s, partner).wait_recv()
        for i in range(2):
            p_copy(0, 1, i).start()
            p_copy(1, 1, i).start()

    def p_turn(k):
        for i in (1, 0):
            for way in range(2):
                if hops(way, k, i):
                    p_wait(way, k, i)
                    if k < 4 and hops(way, k + 1, i):
                        p_copy(way, k + 1, i).start()

    def product(e, i, near):
        if near:
            acc[i] = jnp.zeros((2 * HALF, 512), F32)

        def add(n, carry):
            step = n // 2 + n // 4 if near else 2
            zz = 2 * ((y + step) % 4) + n % 2
            acc[i] += dot_nn(dqbuf[zz], wbuf[zz, e])
            return carry

        lax.fori_loop(0, 6 if near else 2, add, 0)

    def c_copy(u):
        return remote(part_s.at[u], part_r.at[u], c_send.at[u], c_recv.at[u], s, partner)

    def product_other():
        product(1 - xh, 1, False)
        for u in range(2):
            part_s[u] = acc[1, u * HALF:(u + 1) * HALF, :].astype(BF16)
            c_copy(u).start()

    steps["d"] = gather_rows
    steps["q"] = make_piece
    steps["px"] = p_begin
    for k in range(1, 5):
        steps["p%d" % k] = functools.partial(p_turn, k)
    steps["P1a"] = functools.partial(product, xh, 0, True)
    steps["P2a"] = functools.partial(product, xh, 0, False)
    steps["P1b"] = functools.partial(product, 1 - xh, 1, True)
    steps["P2b"] = product_other
    run(5)
    stores = []
    for g in range(KVH):
        lanes = pl.ds(g * HD, HD)
        for i, ref in enumerate((kout_hbm, vout_hbm)):
            stores.append(
                pltpu.make_async_copy(
                    pieces.at[2 * (g % 4) + i, g // 4], ref.at[:, lanes], out_sem.at[2 * g + i]
                )
            )
    stores.append(pltpu.make_async_copy(acc.at[0], own_hbm, out_sem.at[16]))
    for u in range(2):
        stores.append(pltpu.make_async_copy(part_r.at[u], part_hbm.at[u], out_sem.at[17 + u]))
    for store in stores[:17]:
        store.start()
    for u in range(2):
        c_copy(u).wait_recv()
        stores[17 + u].start()

    def kv_done(d, carry):
        kv_out(d).wait_send()
        forward(d).wait_send()
        dkv_out(2 * ((chip + d) % 8) + core).wait_send()
        m_copy(2 * ((chip + d) % 8) + 1 - core).wait_send()
        return carry

    lax.fori_loop(1, 8, kv_done, 0)
    to_sibling.wait_send()
    dkv_out(sibling).wait_send()
    pair_copy.wait_send()
    piece_copy.wait_send()
    for i in range(4):
        x_copy(i).wait_send()

    @pl.when(inner)
    def _():
        for i in range(4):
            on_copy(i).wait_send()

    for u in range(2):
        c_copy(u).wait_send()
        for way in range(2):
            y_copy(u, way).wait_send()
            f_copy(u, way).wait_send()
        for i in range(5):
            s_copy(u, i, core).wait_send()
    for way in range(2):
        for k in range(1, 5):
            for u in range(2):
                if hops(way, k, u):
                    z_copy(way, k, u).wait_send()
                    p_copy(way, k, u).wait_send()
    for store in stores:
        store.wait()


def local(queries, keys, values, grad_attn, segment_ids, q_weight):
    rows, width = queries.shape
    anywhere = pl.BlockSpec(memory_space=pltpu.HBM)
    dma = pltpu.SemaphoreType.DMA
    scratch = [
        pltpu.VMEM((17, 2, HALF, HD), BF16),
        pltpu.VMEM((17, HALF, PER * HALF), F32),
        pltpu.VMEM((17, HALF, PER * HALF), F32),
        pltpu.VMEM((2, PER * HALF, HD), BF16),
        pltpu.VMEM((2, PER * HALF, HD), BF16),
        pltpu.VMEM((2, PER * HALF, HD), F32),
        pltpu.VMEM((8, 8, PER * HALF), F32),
        pltpu.VMEM((16, 2, HALF, HD), BF16),
        pltpu.VMEM((16, 2, HALF, HD), BF16),
        pltpu.VMEM((16, 2, HALF, HD), BF16),
        pltpu.VMEM((2, 2, HALF, HD), F32),
        pltpu.VMEM((2 * HALF, HD), BF16),
        pltpu.VMEM((2 * HALF, HD), BF16),
        pltpu.VMEM((8, 2 * HALF, PER * HD), BF16),
        pltpu.VMEM((8, 2, 2 * HALF, HD), BF16),
        pltpu.VMEM((8, 2, 512, 512), BF16),
        pltpu.VMEM((2, 2 * HALF, 512), F32),
        pltpu.VMEM((2, HALF, 512), BF16),
        pltpu.VMEM((2, HALF, 512), BF16),
        pltpu.VMEM((32, 128), jnp.int32),
    ]
    sizes = (4, 3, 19, 8, 8, 8, 8, 16, 16, 16, 16, 2, 2, 16, 16, 16, 16, 1, 8, 8, 4, 4, 4, 4, 10, 10, 2, 2)
    own, part, key_grad, value_grad = pl.pallas_call(
        attention_kernel,
        out_shape=(
            jax.ShapeDtypeStruct((rows, width), F32),
            jax.ShapeDtypeStruct((2, rows // 2, width), BF16),
            jax.ShapeDtypeStruct((rows, KVH * HD), BF16),
            jax.ShapeDtypeStruct((rows, KVH * HD), BF16),
        ),
        in_specs=[anywhere] * 6,
        out_specs=(anywhere,) * 4,
        scratch_shapes=scratch + [dma((size,)) for size in sizes],
        compiler_params=pltpu.CompilerParams(
            collective_id=0, has_side_effects=True, vmem_limit_bytes=63 * 1024 * 1024
        ),
    )(queries, keys, values, grad_attn, segment_ids.reshape(32, 128), q_weight)
    input_grad = (own + part.reshape(rows, width).astype(F32)).astype(BF16)
    return (input_grad, key_grad, value_grad)


def solution(mesh):
    placed = (
        P("row", "col"),
        P("row", None),
        P("row", None),
        P("row", "col"),
        P(),
        P("row", "col"),
    )
    return jax.shard_map(
        local,
        mesh=mesh,
        in_specs=placed,
        out_specs=(P("row", "col"), P("row", None), P("row", None)),
        check_vma=False,
    )
```

```python
import functools
import math

import jax
import jax.numpy as jnp
from jax import lax
from jax.experimental import pallas as pl
from jax.experimental.pallas import tpu as pltpu
from jax.sharding import PartitionSpec as P

H = 64
KVH = 8
HD = 128
TOKENS = 4096
HALF = 128
PER = 4
NEG = -1e30
PLAN = (
    ("x0", "x1",),
    ("a", "x2",),
    ("x3", "i0",),
    ("i1",),
    ("i2", "i3",),
    ("m", "z1", "o", "b", "Wa", "z2", "d", "z3", "q", "z4", "px", "Wb", "p1", "La", "R1b", "P1b", "Lb", "p2", "R1a", "P1a", "R2b", "P2b", "R2a", "P2a", "p3", "p4",),
)
MESH = pl.DeviceIdType.MESH
INV_ROOT = 1.0 / math.sqrt(HD)
SCALE2 = INV_ROOT * math.log2(math.e)
F32 = jnp.float32
BF16 = jnp.bfloat16


def dot_nt(a, b):
    return lax.dot_general(a, b, (((1,), (1,)), ((), ())), preferred_element_type=F32)


def dot_nn(a, b):
    return lax.dot_general(a, b, (((1,), (0,)), ((), ())), preferred_element_type=F32)


def dot_tn(a, b):
    return lax.dot_general(a, b, (((0,), (0,)), ((), ())), preferred_element_type=F32)


def attention_kernel(
    q_hbm, k_hbm, v_hbm, g_hbm, seg_hbm, w_hbm,
    own_hbm, part_hbm, kout_hbm, vout_hbm,
    kvbuf, sbuf, dpbuf, q4, g4, dq4, stat, pbuf, mbuf, rbuf, ownf, pair_s, pair_r, dqbuf, pieces,
    wbuf, acc, part_s, part_r, seg_ref,
    load_sem, q_sem, out_sem, kv_send, kv_recv, fw_send, fw_recv, m_send, m_recv, dkv_send, dkv_recv, pair_sem,
    xp_sem, z_send, z_recv, p_send, p_recv,
    wl_sem, wx_send, wx_recv, wy_send, wy_recv, wf_send, wf_recv, ws_send, ws_recv, c_send, c_recv,
):
    s = lax.axis_index("row")
    j = lax.axis_index("col")
    chip, core = s // 2, s % 2
    xl, y = chip // 4, chip % 4
    xh, z = j // 8, j % 8
    sibling = s + 1 - 2 * core
    partner = (1 - xh) * 8 + z
    right = xh * 8 + (z + 1) % 8
    left = xh * 8 + (z + 7) % 8
    parity = z % 2
    mate = j + 1 - 2 * parity
    head = j // 2
    inner = xl != xh
    outer = xl == xh

    def remote(src, dst, ssem, rsem, row, col):
        return pltpu.make_async_remote_copy(
            src_ref=src, dst_ref=dst, send_sem=ssem, recv_sem=rsem,
            device_id=(row, col), device_id_type=MESH,
        )

    lanes = pl.ds(pl.multiple_of(head * HD, HD), HD)
    loads = []
    for u in range(2):
        slot = s if u == 0 else 16
        for i, ref in enumerate((k_hbm, v_hbm)):
            loads.append(
                pltpu.make_async_copy(
                    ref.at[pl.ds(u * HALF, HALF), lanes], kvbuf.at[slot, i], load_sem.at[2 * u + i]
                )
            )
    for copy in loads:
        copy.start()
    for u in range(2):
        for h in range(PER):
            for i, (ref, buf) in enumerate(((q_hbm, q4), (g_hbm, g4))):
                pltpu.make_async_copy(
                    ref.at[pl.ds(u * HALF, HALF), pl.ds(h * HD, HD)],
                    buf.at[u, pl.ds(h * HD, HD)],
                    q_sem.at[i],
                ).start()
    seg_load = pltpu.make_async_copy(seg_hbm, seg_ref, q_sem.at[2])
    seg_load.start()

    barrier = pltpu.get_barrier_semaphore()

    def greet(e, carry):
        pl.semaphore_signal(barrier, inc=1, device_id=((s + e) % 16, j), device_id_type=MESH)
        return carry

    lax.fori_loop(1, 16, greet, 0)
    across = (1 - xl) * 8 + y * 2 + core
    for row, col in ((s, right), (s, left), (s, partner), (across, partner)):
        pl.semaphore_signal(barrier, inc=1, device_id=(row, col), device_id_type=MESH)

    seg_load.wait()
    seg = seg_ref[...]
    counts = [jnp.sum((seg < v).astype(F32), keepdims=True) for v in (1, 2, 3)]
    lane = lax.broadcasted_iota(jnp.int32, (1, HALF), 1).astype(F32)
    bounds = []
    for u in range(2):
        block = s if u == 0 else 31 - s
        seg_q = seg_ref[pl.ds(block, 1), :]
        start = jnp.where(
            seg_q == 0, 0.0,
            jnp.where(seg_q == 1, counts[0], jnp.where(seg_q == 2, counts[1], counts[2])),
        )
        stat[4 + u, 0:1, 0:HALF] = start
        stat[4 + u, 1:2, 0:HALF] = lane + (block * HALF).astype(F32)
        stat[u] = jnp.full((8, PER * HALF), NEG, F32)

    for copy in loads:
        copy.wait()
    pltpu.make_async_copy(q4, q4, q_sem.at[0]).wait()
    pltpu.make_async_copy(g4, g4, q_sem.at[1]).wait()
    pl.semaphore_wait(barrier, 19)

    def kv_copy(d, chip_to, row_to):
        src = kvbuf.at[jnp.where(chip_to > chip, s, 16)]
        return remote(src, kvbuf.at[s], kv_send.at[d], kv_recv.at[d], row_to, j)

    def kv_out(d):
        chip_to = (chip + d) % 8
        return kv_copy(d, chip_to, chip_to * 2 + core)

    def kv_start(d, carry):
        kv_out(d).start()
        return carry

    own_half = kvbuf.at[jnp.where(core == 0, s, 16)]
    to_sibling = remote(own_half, kvbuf.at[s], kv_send.at[0], kv_recv.at[0], sibling, j)
    lax.fori_loop(1, 8, kv_start, 0)
    to_sibling.start()

    slot = 2 * y + core
    own_weight = pltpu.make_async_copy(w_hbm, wbuf.at[slot, xh], wl_sem.at[0])

    def quarter(i):
        return pl.ds(i * 128, 128)

    def x_copy(i):
        return remote(
            w_hbm.at[quarter(i)], wbuf.at[slot, xh, quarter(i)],
            wx_send.at[i], wx_recv.at[4 * xh + i], across, xl * 8 + z,
        )

    def on_copy(i):
        ref = wbuf.at[slot, 1 - xh, quarter(i)]
        return remote(ref, ref, wx_send.at[4 + i], wx_recv.at[4 * (1 - xh) + i], across, j)

    def slot_at(step, which):
        return 2 * ((y + step) % 4) + which

    def row_at(step):
        return xl * 8 + ((y + step) % 4) * 2 + core

    def x_wait(e, i):
        ref = wbuf.at[slot, e, quarter(i)]
        remote(ref, ref, wx_send.at[0], wx_recv.at[4 * e + i], across, j).wait_recv()

    def y_copy(e, way):
        ref = wbuf.at[slot, e]
        index = 2 * e + way
        return remote(ref, ref, wy_send.at[index], wy_recv.at[index], row_at(3 if way else 1), j)

    def y_wait(e, way):
        ref = wbuf.at[slot_at(1 if way else 3, core), e]
        index = 2 * e + way
        remote(ref, ref, wy_send.at[index], wy_recv.at[index], s, right).wait_recv()

    def f_ref(step, e, way):
        return wbuf.at[slot_at(step, core), e, pl.ds(way * 256, 256)]

    def f_copy(e, way):
        ref = f_ref(1 if way else 3, e, way)
        index = 2 * e + way
        return remote(ref, ref, wf_send.at[index], wf_recv.at[index], row_at(3 if way else 1), j)

    def f_wait(e, way):
        ref = f_ref(2, e, way)
        index = 2 * e + way
        remote(ref, ref, wf_send.at[index], wf_recv.at[index], s, right).wait_recv()

    def s_copy(e, i, which):
        if i < 3:
            ref = wbuf.at[slot_at((0, 3, 1)[i], which), e]
        else:
            ref = wbuf.at[slot_at(2, which), e, pl.ds((i - 3) * 256, 256)]
        index = 5 * e + i
        return remote(ref, ref, ws_send.at[index], ws_recv.at[index], sibling, j)

    def y_start(e, i, ref):
        for way in range(2):
            index = 2 * e + way
            remote(
                ref, wbuf.at[slot, e, quarter(i)], wy_send.at[index], wy_recv.at[index],
                row_at(3 if way else 1), j,
            ).start()

    steps = {}

    def run(stage):
        for name in PLAN[stage]:
            steps[name]()

    def send_own():
        @pl.when(outer)
        def _():
            own_weight.start()
            for i in range(4):
                y_start(xh, i, w_hbm.at[quarter(i)])

    def weight_inner(i):
        @pl.when(inner)
        def _():
            x_wait(1 - xh, i)
            on_copy(i).start()
            x_wait(xh, i)
            y_start(xh, i, wbuf.at[slot, xh, quarter(i)])
            if i == 3:
                s_copy(xh, 0, core).start()

    def weight_outer():
        @pl.when(outer)
        def _():
            own_weight.wait()
            s_copy(xh, 0, core).start()
            for i in range(4):
                x_wait(1 - xh, i)

    def send_other():
        y_copy(1 - xh, 0).start()
        y_copy(1 - xh, 1).start()
        s_copy(1 - xh, 0, core).start()

    for i in range(4):
        steps["x%d" % i] = x_copy(i).start
        steps["i%d" % i] = functools.partial(weight_inner, i)
    steps["a"] = send_own
    steps["o"] = weight_outer
    steps["b"] = send_other

    def weight_pass(e):
        for way in range(2):
            y_wait(e, way)
            f_copy(e, way).start()
            s_copy(e, 1 + way, core).start()

    def weight_last(e):
        for way in range(2):
            f_wait(e, way)
            s_copy(e, 3 + way, core).start()

    def weight_ready(e, first, last):
        for i in range(first, last):
            s_copy(e, i, 1 - core).wait_recv()

    for name, e in (("a", xh), ("b", 1 - xh)):
        steps["W" + name] = functools.partial(weight_pass, e)
        steps["L" + name] = functools.partial(weight_last, e)
        steps["R1" + name] = functools.partial(weight_ready, e, 0, 3)
        steps["R2" + name] = functools.partial(weight_ready, e, 3, 5)
    run(0)

    sub = lax.broadcasted_iota(jnp.int32, (HALF, HALF), 0).astype(F32)

    def pass_one(t):
        u = jnp.where(t > s, 1, 0)
        block = jnp.where(t > s, jnp.where(t == 16, 31 - s, 31 - t), t)
        key_place = sub + (block * HALF).astype(F32)
        start = stat[4 + u, 0:1, 0:HALF]
        place = stat[4 + u, 1:2, 0:HALF]
        bias = jnp.where((key_place >= start) & (key_place <= place), 0.0, NEG)
        scores = dot_nt(kvbuf[t, 0], q4[u])
        for h in range(PER):
            part = scores[:, h * HALF:(h + 1) * HALF] * SCALE2 + bias
            sbuf[t, :, h * HALF:(h + 1) * HALF] = part
            top = jnp.max(part.reshape(16, 8, HALF), axis=0)
            stat[u, :, h * HALF:(h + 1) * HALF] = jnp.maximum(
                stat[u, :, h * HALF:(h + 1) * HALF], top
            )
        dpbuf[t] = dot_nt(kvbuf[t, 1], g4[u])

    pass_one(s)
    pass_one(16)

    def forward(d):
        origin = ((chip + 8 - d) % 8) * 2 + core
        return remote(kvbuf.at[origin], kvbuf.at[origin], fw_send.at[d], fw_recv.at[d], sibling, j)

    def arrive(d, carry):
        origin = ((chip + 8 - d) % 8) * 2 + core
        remote(
            kvbuf.at[origin], kvbuf.at[origin], kv_send.at[d], kv_recv.at[d], sibling, j
        ).wait_recv()
        forward(d).start()
        pass_one(origin)
        return carry

    lax.fori_loop(1, 8, arrive, 0)

    run(1)
    remote(
        kvbuf.at[sibling], kvbuf.at[sibling], kv_send.at[0], kv_recv.at[0], sibling, j
    ).wait_recv()
    pass_one(sibling)

    def arrive_two(d, carry):
        origin = ((chip + 8 - d) % 8) * 2 + 1 - core
        remote(
            kvbuf.at[origin], kvbuf.at[origin], fw_send.at[d], fw_recv.at[d], sibling, j
        ).wait_recv()
        pass_one(origin)
        return carry

    lax.fori_loop(1, 8, arrive_two, 0)

    run(2)

    for u in range(2):
        top = jnp.max(stat[u], axis=0, keepdims=True)
        stat[u] = jnp.broadcast_to(top, (8, PER * HALF))
        stat[2 + u] = jnp.zeros((8, PER * HALF), F32)
        stat[6 + u] = jnp.zeros((8, PER * HALF), F32)

    def pass_two(t, carry):
        u = jnp.where(t > s, 1, 0)
        for h in range(PER):
            cols = slice(h * HALF, (h + 1) * HALF)
            top = stat[u, 0:1, cols]
            expo = jnp.exp2(sbuf[t, :, cols] - top)
            sbuf[t, :, cols] = expo
            stat[2 + u, :, cols] += jnp.sum(expo.reshape(16, 8, HALF), axis=0)
            stat[6 + u, :, cols] += jnp.sum((expo * dpbuf[t, :, cols]).reshape(16, 8, HALF), axis=0)
        return carry

    lax.fori_loop(0, 17, pass_two, 0)

    run(3)
    for u in range(2):
        total = jnp.sum(stat[2 + u], axis=0, keepdims=True)
        inverse = 1.0 / total
        delta = jnp.sum(stat[6 + u], axis=0, keepdims=True) * inverse
        stat[2 + u, 0:1, :] = inverse
        stat[6 + u, 0:1, :] = delta
        dq4[u] = jnp.zeros((PER * HALF, HD), F32)

    def m_copy(t):
        return remote(pbuf.at[t], mbuf.at[t], m_send.at[t], m_recv.at[t], sibling, j)

    def dkv_out(t):
        return remote(pbuf.at[t], rbuf.at[s], dkv_send.at[t], dkv_recv.at[s], t, j)

    def pass_three(t, carry):
        u = jnp.where(t > s, 1, 0)
        inverse = stat[2 + u, 0:1, :]
        delta = stat[6 + u, 0:1, :]
        probs = sbuf[t] * inverse
        dscore = (probs * (dpbuf[t] - delta)).astype(BF16)
        key_part = dot_nn(dscore, q4[u])
        value_part = dot_nn(probs.astype(BF16), g4[u])
        dq4[u] += dot_tn(dscore, kvbuf[t, 0])
        mine = (t == s) | (t == 16)

        @pl.when(mine)
        def _():
            ownf[u, 0] = key_part
            ownf[u, 1] = value_part

        @pl.when(jnp.logical_not(mine))
        def _():
            pbuf[t, 0] = key_part.astype(BF16)
            pbuf[t, 1] = value_part.astype(BF16)

            @pl.when(t == sibling)
            def _():
                dkv_out(t).start()

            @pl.when((t != sibling) & (t % 2 != core))
            def _():
                m_copy(t).start()

        return carry

    def z_copy(way, k, u):
        origin = (z + 8 - (k - 1)) % 8 if way == 0 else (z + (k - 1)) % 8
        src = dqbuf.at[origin, pl.ds(u * HALF, HALF)]
        index = (way * 4 + (k - 1)) * 2 + u
        return remote(src, src, z_send.at[index], z_recv.at[index], s, right if way == 0 else left)

    def z_wait(way, k, u):
        origin = (z + 8 - k) % 8 if way == 0 else (z + k) % 8
        dst = dqbuf.at[origin, pl.ds(u * HALF, HALF)]
        index = (way * 4 + (k - 1)) * 2 + u
        remote(dst, dst, z_send.at[index], z_recv.at[index], s, right).wait_recv()

    def hops(way, k, u):
        return k <= 3 or u == way

    def z_turn(k):
        for u in (1, 0):
            for way in range(2):
                if hops(way, k, u):
                    z_wait(way, k, u)
                    if k < 4 and hops(way, k + 1, u):
                        z_copy(way, k + 1, u).start()

    for u, first, last in ((1, s + 1, 17), (0, 0, s + 1)):
        lax.fori_loop(first, last, pass_three, 0)
        for h in range(PER):
            dqbuf[z, u * HALF:(u + 1) * HALF, h * HD:(h + 1) * HD] = (
                dq4[u, h * HD:(h + 1) * HD, :] * INV_ROOT
            ).astype(BF16)
        z_copy(0, 1, u).start()
        z_copy(1, 1, u).start()
        if u == 1:
            run(4)

    def merge(d, carry):
        t = 2 * ((chip + d) % 8) + core
        remote(pbuf.at[t], mbuf.at[t], m_send.at[t], m_recv.at[t], sibling, j).wait_recv()
        for i in range(2):
            pbuf[t, i] = (pbuf[t, i].astype(F32) + mbuf[t, i].astype(F32)).astype(BF16)
        dkv_out(t).start()
        return carry

    steps["m"] = lambda: lax.fori_loop(1, 8, merge, 0)
    for k in range(1, 5):
        steps["z%d" % k] = functools.partial(z_turn, k)

    def dkv_take(r):
        remote(rbuf.at[r], rbuf.at[r], dkv_send.at[r], dkv_recv.at[r], s, right).wait_recv()
        u = jnp.where(r > s, 0, 1)
        for i in range(2):
            ownf[u, i] += rbuf[r, i].astype(F32)

    def take(d, carry):
        dkv_take(2 * ((chip + 8 - d) % 8) + core)
        return carry

    pair_copy = remote(pair_s, pair_r, pair_sem.at[0], pair_sem.at[1], s, mate)
    piece = pieces.at[z, xh]
    piece_copy = remote(piece, piece, xp_sem.at[0], xp_sem.at[1], s, partner)

    def gather_rows():
        dkv_take(sibling)
        lax.fori_loop(1, 8, take, 0)
        for u in range(2):
            pair_s[u * HALF:(u + 1) * HALF, :] = ownf[u, 1 - parity].astype(BF16)
        pair_copy.start()

    def make_piece():
        pair_copy.wait_recv()
        factor = jnp.where(parity == 0, INV_ROOT, 1.0).astype(F32)
        for u in range(2):
            rows = slice(u * HALF, (u + 1) * HALF)
            pieces[z, xh, rows, :] = (
                (ownf[u, parity] + pair_r[rows, :].astype(F32)) * factor
            ).astype(BF16)
        piece_copy.start()

    def p_copy(way, k, i):
        origin = (z + 8 - (k - 1)) % 8 if way == 0 else (z + (k - 1)) % 8
        src = pieces.at[origin, i]
        index = (way * 4 + (k - 1)) * 2 + i
        return remote(src, src, p_send.at[index], p_recv.at[index], s, right if way == 0 else left)

    def p_wait(way, k, i):
        origin = (z + 8 - k) % 8 if way == 0 else (z + k) % 8
        dst = pieces.at[origin, i]
        index = (way * 4 + (k - 1)) * 2 + i
        remote(dst, dst, p_send.at[index], p_recv.at[index], s, right).wait_recv()

    def p_begin():
        other = pieces.at[z, 1 - xh]
        remote(other, other, xp_sem.at[0], xp_sem.at[1], s, partner).wait_recv()
        for i in range(2):
            p_copy(0, 1, i).start()
            p_copy(1, 1, i).start()

    def p_turn(k):
        for i in (1, 0):
            for way in range(2):
                if hops(way, k, i):
                    p_wait(way, k, i)
                    if k < 4 and hops(way, k + 1, i):
                        p_copy(way, k + 1, i).start()

    def product(e, i, near):
        if near:
            acc[i] = jnp.zeros((2 * HALF, 512), F32)

        def add(n, carry):
            step = n // 2 + n // 4 if near else 2
            zz = 2 * ((y + step) % 4) + n % 2
            acc[i] += dot_nn(dqbuf[zz], wbuf[zz, e])
            return carry

        lax.fori_loop(0, 6 if near else 2, add, 0)

    def c_copy(u):
        return remote(part_s.at[u], part_r.at[u], c_send.at[u], c_recv.at[u], s, partner)

    def product_other():
        product(1 - xh, 1, False)
        for u in range(2):
            part_s[u] = acc[1, u * HALF:(u + 1) * HALF, :].astype(BF16)
            c_copy(u).start()

    steps["d"] = gather_rows
    steps["q"] = make_piece
    steps["px"] = p_begin
    for k in range(1, 5):
        steps["p%d" % k] = functools.partial(p_turn, k)
    steps["P1a"] = functools.partial(product, xh, 0, True)
    steps["P2a"] = functools.partial(product, xh, 0, False)
    steps["P1b"] = functools.partial(product, 1 - xh, 1, True)
    steps["P2b"] = product_other
    run(5)
    stores = []
    for g in range(KVH):
        lanes = pl.ds(g * HD, HD)
        for i, ref in enumerate((kout_hbm, vout_hbm)):
            stores.append(
                pltpu.make_async_copy(
                    pieces.at[2 * (g % 4) + i, g // 4], ref.at[:, lanes], out_sem.at[2 * g + i]
                )
            )
    stores.append(pltpu.make_async_copy(acc.at[0], own_hbm, out_sem.at[16]))
    for u in range(2):
        stores.append(pltpu.make_async_copy(part_r.at[u], part_hbm.at[u], out_sem.at[17 + u]))
    for store in stores[:17]:
        store.start()
    for u in range(2):
        c_copy(u).wait_recv()
        stores[17 + u].start()

    def kv_done(d, carry):
        kv_out(d).wait_send()
        forward(d).wait_send()
        dkv_out(2 * ((chip + d) % 8) + core).wait_send()
        m_copy(2 * ((chip + d) % 8) + 1 - core).wait_send()
        return carry

    lax.fori_loop(1, 8, kv_done, 0)
    to_sibling.wait_send()
    dkv_out(sibling).wait_send()
    pair_copy.wait_send()
    piece_copy.wait_send()
    for i in range(4):
        x_copy(i).wait_send()

    @pl.when(inner)
    def _():
        for i in range(4):
            on_copy(i).wait_send()

    for u in range(2):
        c_copy(u).wait_send()
        for way in range(2):
            y_copy(u, way).wait_send()
            f_copy(u, way).wait_send()
        for i in range(5):
            s_copy(u, i, core).wait_send()
    for way in range(2):
        for k in range(1, 5):
            for u in range(2):
                if hops(way, k, u):
                    z_copy(way, k, u).wait_send()
                    p_copy(way, k, u).wait_send()
    for store in stores:
        store.wait()


def local(queries, keys, values, grad_attn, segment_ids, q_weight):
    rows, width = queries.shape
    anywhere = pl.BlockSpec(memory_space=pltpu.HBM)
    dma = pltpu.SemaphoreType.DMA
    scratch = [
        pltpu.VMEM((17, 2, HALF, HD), BF16),
        pltpu.VMEM((17, HALF, PER * HALF), F32),
        pltpu.VMEM((17, HALF, PER * HALF), F32),
        pltpu.VMEM((2, PER * HALF, HD), BF16),
        pltpu.VMEM((2, PER * HALF, HD), BF16),
        pltpu.VMEM((2, PER * HALF, HD), F32),
        pltpu.VMEM((8, 8, PER * HALF), F32),
        pltpu.VMEM((16, 2, HALF, HD), BF16),
        pltpu.VMEM((16, 2, HALF, HD), BF16),
        pltpu.VMEM((16, 2, HALF, HD), BF16),
        pltpu.VMEM((2, 2, HALF, HD), F32),
        pltpu.VMEM((2 * HALF, HD), BF16),
        pltpu.VMEM((2 * HALF, HD), BF16),
        pltpu.VMEM((8, 2 * HALF, PER * HD), BF16),
        pltpu.VMEM((8, 2, 2 * HALF, HD), BF16),
        pltpu.VMEM((8, 2, 512, 512), BF16),
        pltpu.VMEM((2, 2 * HALF, 512), F32),
        pltpu.VMEM((2, HALF, 512), BF16),
        pltpu.VMEM((2, HALF, 512), BF16),
        pltpu.VMEM((32, 128), jnp.int32),
    ]
    sizes = (4, 3, 19, 8, 8, 8, 8, 16, 16, 16, 16, 2, 2, 16, 16, 16, 16, 1, 8, 8, 4, 4, 4, 4, 10, 10, 2, 2)
    own, part, key_grad, value_grad = pl.pallas_call(
        attention_kernel,
        out_shape=(
            jax.ShapeDtypeStruct((rows, width), F32),
            jax.ShapeDtypeStruct((2, rows // 2, width), BF16),
            jax.ShapeDtypeStruct((rows, KVH * HD), BF16),
            jax.ShapeDtypeStruct((rows, KVH * HD), BF16),
        ),
        in_specs=[anywhere] * 6,
        out_specs=(anywhere,) * 4,
        scratch_shapes=scratch + [dma((size,)) for size in sizes],
        compiler_params=pltpu.CompilerParams(
            collective_id=0, has_side_effects=True, vmem_limit_bytes=63 * 1024 * 1024
        ),
    )(queries, keys, values, grad_attn, segment_ids.reshape(32, 128), q_weight)
    input_grad = (own + part.reshape(rows, width).astype(F32)).astype(BF16)
    return (input_grad, key_grad, value_grad)


def solution(mesh):
    placed = (
        P("row", "col"),
        P("row", None),
        P("row", None),
        P("row", "col"),
        P(),
        P("row", "col"),
    )
    return jax.shard_map(
        local,
        mesh=mesh,
        in_specs=placed,
        out_specs=(P("row", "col"), P("row", None), P("row", None)),
        check_vma=False,
    )
```
